32 devices in a mesh: groups: 2 (over x), section: 16 (over z, y, core).
Axes of the slice: x: 2, y: 2, z: 4, core: 2. Of those that a mesh axis runs over, the one named last changes fastest.
Arguments:
- latent_rows: bfloat16 [32, 256, 1408], P(('groups', 'section')), parts along dimension 0, may hold values from -6 to 6
- skip_queue: bfloat16 [32, 256, 1408], P(('groups', 'section')), parts along dimension 0, may hold values from -6 to 6
- norm_gain: float32 [16, 1408], P('section'), may hold values from 0.1 to 1.9
- skip_weight: bfloat16 [16, 2816, 1408], P('section'), may hold values from -0.109375 to 0.109375
- up_weight: bfloat16 [16, 1408, 3072], P('section'), may hold values from -0.15625 to 0.15625
- down_weight: bfloat16 [16, 3072, 1408], P('section'), may hold values from -0.109375 to 0.109375
Outputs:
- next_rows: bfloat16 [32, 256, 1408], P(('groups', 'section')), parts along dimension 0
- next_queue: bfloat16 [32, 256, 1408], P(('groups', 'section')), parts along dimension 0
The draws below stay inside these ranges and needn't reach their ends.
There are 2 independent parts, one for each index of `groups`. The reference program is written for one: setup_inputs(seed, part) draws one part's arguments, and reference() takes and returns one part's arrays. A program takes and returns all parts, laid end to end along the dimension named above; an argument that names none is the same for every part. Nothing has to cross between parts.
All inputs are finite; a program needn't handle non-finite values.
Results may differ from the reference program's by a relative error of at most 0.008.
Values may be sent and summed in bfloat16 or wider, within the bound.
A program may use at most 128 MiB of HBM per device.

```python
import jax
import jax.numpy as jnp
from jax import lax

D = 1408
FFW = 3072
TICKS = 3
SECTIONS = 16
ROWS = 256


def steps_of(stream_key, extent, pieces, low, largest):
    level = 1.0
    for position, shards_of in pieces:
        heights = jax.random.uniform(jax.random.fold_in(jax.random.fold_in(stream_key, 6), position), (shards_of,), jnp.float32, low / len(pieces), largest / len(pieces))
        level = level * jnp.repeat(jnp.exp(heights), extent[position] // shards_of).reshape((-1,) + (1,) * (len(extent) - 1 - position))
    return level


def scatter_about(rng, dims, width, bound, cuts=(), held_as=jnp.bfloat16):
    entries = width * jax.random.normal(rng, dims, jnp.float32)
    if cuts:
        entries = entries * steps_of(rng, dims, cuts, -0.22, 0.18)
    return jnp.clip(entries, -bound, bound).astype(held_as)


def setup_inputs(seed: int = 0, part: int = 0) -> dict:
    arg_keys = jax.random.split(jax.random.key(seed), 7)
    part_splits = jax.random.split(jax.random.fold_in(arg_keys[6], part), 7)
    return {
        "latent_rows": scatter_about(part_splits[0], (SECTIONS, ROWS, D), 1.0, 6.0, ((0, 16),)),
        "skip_queue": scatter_about(part_splits[1], (SECTIONS, ROWS, D), 1.0, 6.0, ((0, 16),)),
        "norm_gain": jnp.clip(1.0 + 0.18 * jax.random.normal(arg_keys[2], (SECTIONS, D), jnp.float32), 0.1, 1.9),
        "skip_weight": scatter_about(arg_keys[3], (SECTIONS, 2 * D, D), (2 * D) ** -0.5, 0.109375, ((0, 16),)),
        "up_weight": scatter_about(arg_keys[4], (SECTIONS, D, FFW), D ** -0.5, 0.15625, ((0, 16),)),
        "down_weight": scatter_about(arg_keys[5], (SECTIONS, FFW, D), FFW ** -0.5, 0.109375, ((0, 16),)),
    }


epsilon = 1e-06

def block(items):
    current, queue_row, decoder, gain, merging, upper, lower = items
    joined = jnp.concatenate([current, queue_row], axis=1)
    mixed = jnp.dot(joined, merging, preferred_element_type=jnp.float32)
    merged = jnp.where(decoder, mixed, current.astype(jnp.float32))
    center = lax.optimization_barrier(jnp.mean(merged, axis=1, keepdims=True))
    spread = lax.optimization_barrier(jnp.mean(jnp.square(merged - center), axis=1, keepdims=True))
    normed = ((merged - center) * lax.rsqrt(spread + epsilon) * gain).astype(jnp.bfloat16)
    hidden = jax.nn.gelu(jnp.dot(normed, upper, preferred_element_type=jnp.float32), approximate=True).astype(jnp.bfloat16)
    return (merged + jnp.dot(hidden, lower, preferred_element_type=jnp.float32)).astype(jnp.bfloat16)

def reference(latent_rows, skip_queue, norm_gain, skip_weight, up_weight, down_weight):
    sections = latent_rows.shape[0]
    halfway = sections // 2
    decoder_flags = jnp.arange(sections) >= halfway
    current = latent_rows
    queue_now = skip_queue
    for repeat in range(TICKS):
        output = lax.map(block, (current, queue_now, decoder_flags, norm_gain, skip_weight, up_weight, down_weight))
        current = jnp.concatenate([output[-1:], output[:-1]], axis=0)
        queue_now = jnp.concatenate([output[:halfway], queue_now[:halfway][::-1]], axis=0)
    return (current, queue_now)
```

```python
import functools

import jax
import jax.numpy as jnp
from jax import lax
from jax.experimental import pallas as pl
from jax.experimental.pallas import tpu as pltpu
from jax.sharding import PartitionSpec as P

TICKS = 3


epsilon = 1e-06

MESH = pl.DeviceIdType.MESH


def tile_of(extent, choices):
    return next((c for c in choices if extent % c == 0), extent)


def kernel(
    sections,
    rows_hbm,
    queue_hbm,
    gain_ref,
    skip_hbm,
    up_hbm,
    down_hbm,
    next_rows_ref,
    next_queue_ref,
    skip_ref,
    up_ref,
    down_ref,
    rows_in,
    queue_in,
    outputs,
    total,
    normed,
    load_sem,
    queue_send,
    queue_recv,
    rows_send,
    rows_recv,
    hold_sem,
    relay,
    relay_send,
    relay_recv,
):
    me = lax.axis_index("section")
    half = sections // 2
    right = lax.rem(me + 1, sections)
    left = lax.rem(me + sections - 1, sections)
    mirror = sections - 1 - me
    encoder = me < half
    decoder = me >= half
    far = jnp.logical_and(me < half // 2, lax.rem(me, 2) == 1)
    near = jnp.logical_and(encoder, jnp.logical_not(far))
    row_count, width = rows_hbm.shape[1:]
    hidden_width = up_ref.shape[1]

    load_up = pltpu.make_async_copy(up_hbm.at[0], up_ref, load_sem.at[0])
    load_down = pltpu.make_async_copy(down_hbm.at[0], down_ref, load_sem.at[1])
    load_rows = pltpu.make_async_copy(rows_hbm.at[0], rows_in.at[0], load_sem.at[2])
    load_skip = pltpu.make_async_copy(skip_hbm.at[0], skip_ref, load_sem.at[3])
    load_queue = pltpu.make_async_copy(queue_hbm.at[0], queue_in.at[0], load_sem.at[4])

    leader = half - 1
    holders = [s for s in range(half - 1) if (s // 2 - leader // 2) % 2 == 0 or s < half // 2]
    shares = jnp.logical_or(lax.rem(me // 2 + leader // 2, 2) == 0, me < half // 2)
    holds = jnp.logical_and(me < leader, shares)

    helper = leader - 2
    relayed = relay.shape[0]
    first, rest = pl.ds(0, relayed), pl.ds(relayed, row_count - relayed)

    def relay_copy(hop):
        return pltpu.make_async_remote_copy(
            src_ref=relay if hop else outputs.at[TICKS - 1, first],
            dst_ref=next_rows_ref.at[0, first] if hop else relay,
            send_sem=relay_send,
            recv_sem=relay_recv,
            device_id={"section": half if hop else helper},
            device_id_type=MESH,
        )

    direct_copy = pltpu.make_async_remote_copy(
        src_ref=outputs.at[TICKS - 1, rest],
        dst_ref=next_rows_ref.at[0, rest],
        send_sem=rows_send.at[TICKS - 1],
        recv_sem=rows_recv.at[TICKS - 1],
        device_id={"section": half},
        device_id_type=MESH,
    )

    def queue_copy(tick):
        source = queue_hbm.at[0] if tick == 0 else outputs.at[tick - 1]
        return pltpu.make_async_remote_copy(
            src_ref=source,
            dst_ref=next_queue_ref.at[0] if tick == TICKS - 1 else queue_in.at[tick + 1],
            send_sem=queue_send.at[tick],
            recv_sem=queue_recv.at[tick],
            device_id={"section": mirror},
            device_id_type=MESH,
        )

    def rows_copy(tick):
        return pltpu.make_async_remote_copy(
            src_ref=outputs.at[tick],
            dst_ref=next_rows_ref.at[0] if tick == TICKS - 1 else rows_in.at[tick + 1],
            send_sem=rows_send.at[tick],
            recv_sem=rows_recv.at[tick],
            device_id={"section": right},
            device_id_type=MESH,
        )

    barrier = pltpu.get_barrier_semaphore()
    pl.semaphore_signal(barrier, inc=1, device_id={"section": left}, device_id_type=MESH)

    @pl.when(decoder)
    def _():
        pl.semaphore_signal(barrier, inc=1, device_id={"section": mirror}, device_id_type=MESH)

    @pl.when(holds)
    def _():
        pl.semaphore_signal(barrier, inc=1, device_id={"section": leader}, device_id_type=MESH)

    @pl.when(me == half)
    def _():
        pl.semaphore_signal(barrier, inc=1, device_id={"section": helper}, device_id_type=MESH)

    @pl.when(me == helper)
    def _():
        pl.semaphore_signal(barrier, inc=1, device_id={"section": leader}, device_id_type=MESH)
        pl.semaphore_wait(barrier, 3)

    @pl.when(me == leader)
    def _():
        pl.semaphore_wait(barrier, 3 + len(holders))

    @pl.when(jnp.logical_and(encoder, jnp.logical_and(me != leader, me != helper)))
    def _():
        pl.semaphore_wait(barrier, 2)

    @pl.when(decoder)
    def _():
        pl.semaphore_wait(barrier, 1)

    @pl.when(near)
    def _():
        queue_copy(0).start()

    load_rows.start()
    load_up.start()
    load_down.start()

    @pl.when(decoder)
    def _():
        load_queue.start()
        load_skip.start()

    for tick in range(TICKS):
        if tick == 0:
            load_rows.wait()

            @pl.when(decoder)
            def _():
                load_queue.wait()
                load_skip.wait()
        else:
            @pl.when(me != half)
            def _():
                rows_copy(tick - 1).wait_recv()

            if tick == 1:

                @pl.when(decoder)
                def _():
                    queue_copy(0).wait_recv()
            else:

                @pl.when(me > half)
                def _():
                    queue_copy(tick - 1).wait_recv()

            @pl.when(me == half)
            def _():
                queue_copy(tick).wait_recv()
                rows_in[tick] = next_queue_ref[0] if tick == TICKS - 1 else queue_in[tick + 1]

        @pl.when(encoder)
        def _():
            total[...] = rows_in[tick].astype(jnp.float32)

        @pl.when(decoder)
        def _():
            def merge(start, size):
                columns = pl.ds(start, size)
                total[:, columns] = jnp.dot(
                    rows_in[tick], skip_ref[:width, columns], preferred_element_type=jnp.float32
                ) + jnp.dot(
                    queue_in[tick], skip_ref[width:, columns], preferred_element_type=jnp.float32
                )

            whole = width // 256

            @pl.loop(0, whole)
            def _(i):
                merge(pl.multiple_of(i * 256, 256), 256)

            if width % 256:
                merge(whole * 256, width % 256)

        band = tile_of(row_count, (32, 16))

        @pl.loop(0, row_count // band)
        def _(i):
            part = pl.ds(pl.multiple_of(i * band, band), band)
            merged = total[part, :]
            center = jnp.mean(merged, axis=1, keepdims=True)
            spread = jnp.mean(jnp.square(merged - center), axis=1, keepdims=True)
            normed[part, :] = (
                (merged - center) * lax.rsqrt(spread + epsilon) * gain_ref[...]
            ).astype(jnp.bfloat16)

        if tick == 0:
            load_up.wait()
            load_down.wait()

        step = tile_of(hidden_width, (512, 256, 128))

        @pl.loop(0, hidden_width // step)
        def _(i):
            part = pl.ds(pl.multiple_of(i * step, step), step)
            hidden = jax.nn.gelu(
                jnp.dot(normed[...], up_ref[:, part], preferred_element_type=jnp.float32),
                approximate=True,
            ).astype(jnp.bfloat16)
            total[...] += jnp.dot(hidden, down_ref[part, :], preferred_element_type=jnp.float32)

        outputs[tick] = total[...].astype(jnp.bfloat16)

        if tick < TICKS - 1:

            @pl.when(me != half - 1)
            def _():
                rows_copy(tick).start()

            if tick == 0:

                @pl.when(far)
                def _():
                    queue_copy(0).start()

            now = encoder if tick < TICKS - 2 else jnp.logical_and(encoder, jnp.logical_not(holds))

            @pl.when(now)
            def _():
                queue_copy(tick + 1).start()
        else:

            @pl.when(me != leader)
            def _():
                rows_copy(tick).start()

            @pl.when(me == leader)
            def _():
                relay_copy(0).start()
                direct_copy.start()

    @pl.when(encoder)
    def _():
        next_queue_ref[0] = outputs[TICKS - 1]

    @pl.when(me == leader)
    def _():
        queue_copy(TICKS - 1).wait_send()
        for peer in holders:
            pl.semaphore_signal(hold_sem, inc=1, device_id={"section": peer}, device_id_type=MESH)

    @pl.when(holds)
    def _():
        pl.semaphore_wait(hold_sem, 1)
        queue_copy(TICKS - 1).start()

    @pl.when(me == helper)
    def _():
        relay_copy(0).wait_recv()
        relay_copy(1).start()

    @pl.when(me != half)
    def _():
        rows_copy(TICKS - 1).wait_recv()

    @pl.when(me == half)
    def _():
        direct_copy.wait_recv()
        relay_copy(1).wait_recv()

    @pl.when(me > half)
    def _():
        queue_copy(TICKS - 1).wait_recv()

    for tick in range(TICKS):
        unsent = encoder if tick < TICKS - 1 else jnp.logical_and(encoder, me != leader)

        @pl.when(unsent)
        def _():
            queue_copy(tick).wait_send()

        if tick < TICKS - 1:

            @pl.when(me != half - 1)
            def _():
                rows_copy(tick).wait_send()
        else:

            @pl.when(me != leader)
            def _():
                rows_copy(tick).wait_send()

            @pl.when(me == leader)
            def _():
                relay_copy(0).wait_send()
                direct_copy.wait_send()

    @pl.when(me == helper)
    def _():
        relay_copy(1).wait_send()


def local(latent_rows, skip_queue, norm_gain, skip_weight, up_weight, down_weight):
    sections = lax.axis_size("section")
    _, row_count, width = latent_rows.shape
    hidden_width = up_weight.shape[2]
    shape = jax.ShapeDtypeStruct(latent_rows.shape, jnp.bfloat16)
    in_hbm = pl.BlockSpec(memory_space=pltpu.HBM)
    in_vmem = pl.BlockSpec(memory_space=pltpu.VMEM)
    return pl.pallas_call(
        functools.partial(kernel, sections),
        out_shape=(shape, shape),
        in_specs=[in_hbm, in_hbm, in_vmem, in_hbm, in_hbm, in_hbm],
        out_specs=(in_vmem, in_vmem),
        scratch_shapes=[
            pltpu.VMEM((2 * width, width), jnp.bfloat16),
            pltpu.VMEM((width, hidden_width), jnp.bfloat16),
            pltpu.VMEM((hidden_width, width), jnp.bfloat16),
            pltpu.VMEM((TICKS, row_count, width), jnp.bfloat16),
            pltpu.VMEM((TICKS, row_count, width), jnp.bfloat16),
            pltpu.VMEM((TICKS, row_count, width), jnp.bfloat16),
            pltpu.VMEM((row_count, width), jnp.float32),
            pltpu.VMEM((row_count, width), jnp.bfloat16),
            pltpu.SemaphoreType.DMA((5,)),
            pltpu.SemaphoreType.DMA((TICKS,)),
            pltpu.SemaphoreType.DMA((TICKS,)),
            pltpu.SemaphoreType.DMA((TICKS,)),
            pltpu.SemaphoreType.DMA((TICKS,)),
            pltpu.SemaphoreType.REGULAR,
            pltpu.VMEM((row_count // 2, width), jnp.bfloat16),
            pltpu.SemaphoreType.DMA,
            pltpu.SemaphoreType.DMA,
        ],
        compiler_params=pltpu.CompilerParams(
            collective_id=0, has_side_effects=True, vmem_limit_bytes=52 << 20
        ),
    )(latent_rows, skip_queue, norm_gain, skip_weight, up_weight, down_weight)


def solution(mesh):
    return jax.shard_map(
        local,
        mesh=mesh,
        in_specs=(
            P(("groups", "section"), None, None),
            P(("groups", "section"), None, None),
            P("section", None),
            P("section", None, None),
            P("section", None, None),
            P("section", None, None),
        ),
        out_specs=(P(("groups", "section"), None, None), P(("groups", "section"), None, None)),
        check_vma=False,
    )
```

```python
import functools

import jax
import jax.numpy as jnp
from jax import lax
from jax.experimental import pallas as pl
from jax.experimental.pallas import tpu as pltpu
from jax.sharding import PartitionSpec as P

TICKS = 3


epsilon = 1e-06

MESH = pl.DeviceIdType.MESH


def spans(extent, step):
    return [(start, min(step, extent - start)) for start in range(0, extent, step)]


def kernel(
    sections,
    rows_hbm,
    queue_hbm,
    gain_ref,
    skip_hbm,
    up_hbm,
    down_hbm,
    next_rows_ref,
    next_queue_ref,
    skip_ref,
    up_ref,
    down_ref,
    rows_in,
    queue_in,
    outputs,
    total,
    normed,
    hidden,
    load_sem,
    queue_send,
    queue_recv,
    rows_send,
    rows_recv,
    hold_sem,
    relay,
    relay_send,
    relay_recv,
):
    me = lax.axis_index("section")
    half = sections // 2
    right = lax.rem(me + 1, sections)
    left = lax.rem(me + sections - 1, sections)
    mirror = sections - 1 - me
    encoder = me < half
    decoder = me >= half
    far = jnp.logical_and(me < half // 2, lax.rem(me, 2) == 1)
    near = jnp.logical_and(encoder, jnp.logical_not(far))
    row_count, width = rows_hbm.shape[1:]
    hidden_width = up_ref.shape[1]

    load_up = pltpu.make_async_copy(up_hbm.at[0], up_ref, load_sem.at[0])
    load_down = pltpu.make_async_copy(down_hbm.at[0], down_ref, load_sem.at[1])
    load_rows = pltpu.make_async_copy(rows_hbm.at[0], rows_in.at[0], load_sem.at[2])
    load_skip = pltpu.make_async_copy(skip_hbm.at[0], skip_ref, load_sem.at[3])
    load_queue = pltpu.make_async_copy(queue_hbm.at[0], queue_in.at[0], load_sem.at[4])

    leader = half - 1
    holders = [s for s in range(half - 1) if (s // 2 - leader // 2) % 2 == 0 or s < half // 2]
    shares = jnp.logical_or(lax.rem(me // 2 + leader // 2, 2) == 0, me < half // 2)
    holds = jnp.logical_and(me < leader, shares)

    helper = leader - 2
    relayed = relay.shape[0]
    first, rest = pl.ds(0, relayed), pl.ds(relayed, row_count - relayed)

    def relay_copy(hop):
        return pltpu.make_async_remote_copy(
            src_ref=relay if hop else outputs.at[TICKS - 1, first],
            dst_ref=next_rows_ref.at[0, first] if hop else relay,
            send_sem=relay_send,
            recv_sem=relay_recv,
            device_id={"section": half if hop else helper},
            device_id_type=MESH,
        )

    direct_copy = pltpu.make_async_remote_copy(
        src_ref=outputs.at[TICKS - 1, rest],
        dst_ref=next_rows_ref.at[0, rest],
        send_sem=rows_send.at[TICKS - 1],
        recv_sem=rows_recv.at[TICKS - 1],
        device_id={"section": half},
        device_id_type=MESH,
    )

    def queue_copy(tick):
        source = queue_hbm.at[0] if tick == 0 else outputs.at[tick - 1]
        return pltpu.make_async_remote_copy(
            src_ref=source,
            dst_ref=next_queue_ref.at[0] if tick == TICKS - 1 else queue_in.at[tick + 1],
            send_sem=queue_send.at[tick],
            recv_sem=queue_recv.at[tick],
            device_id={"section": mirror},
            device_id_type=MESH,
        )

    def rows_copy(tick):
        return pltpu.make_async_remote_copy(
            src_ref=outputs.at[tick],
            dst_ref=next_rows_ref.at[0] if tick == TICKS - 1 else rows_in.at[tick + 1],
            send_sem=rows_send.at[tick],
            recv_sem=rows_recv.at[tick],
            device_id={"section": right},
            device_id_type=MESH,
        )

    barrier = pltpu.get_barrier_semaphore()
    pl.semaphore_signal(barrier, inc=1, device_id={"section": left}, device_id_type=MESH)

    @pl.when(decoder)
    def _():
        pl.semaphore_signal(barrier, inc=1, device_id={"section": mirror}, device_id_type=MESH)

    @pl.when(holds)
    def _():
        pl.semaphore_signal(barrier, inc=1, device_id={"section": leader}, device_id_type=MESH)

    @pl.when(me == half)
    def _():
        pl.semaphore_signal(barrier, inc=1, device_id={"section": helper}, device_id_type=MESH)

    @pl.when(me == helper)
    def _():
        pl.semaphore_signal(barrier, inc=1, device_id={"section": leader}, device_id_type=MESH)
        pl.semaphore_wait(barrier, 3)

    @pl.when(me == leader)
    def _():
        pl.semaphore_wait(barrier, 3 + len(holders))

    @pl.when(jnp.logical_and(encoder, jnp.logical_and(me != leader, me != helper)))
    def _():
        pl.semaphore_wait(barrier, 2)

    @pl.when(decoder)
    def _():
        pl.semaphore_wait(barrier, 1)

    @pl.when(near)
    def _():
        queue_copy(0).start()

    load_rows.start()
    load_up.start()
    load_down.start()

    @pl.when(decoder)
    def _():
        load_queue.start()
        load_skip.start()

    for tick in range(TICKS):
        if tick == 0:
            load_rows.wait()

            @pl.when(decoder)
            def _():
                load_queue.wait()
                load_skip.wait()
        else:
            @pl.when(me != half)
            def _():
                rows_copy(tick - 1).wait_recv()

            if tick == 1:

                @pl.when(decoder)
                def _():
                    queue_copy(0).wait_recv()
            else:

                @pl.when(me > half)
                def _():
                    queue_copy(tick - 1).wait_recv()

            @pl.when(me == half)
            def _():
                queue_copy(tick).wait_recv()
                rows_in[tick] = next_queue_ref[0] if tick == TICKS - 1 else queue_in[tick + 1]

        @pl.when(encoder)
        def _():
            total[...] = rows_in[tick].astype(jnp.float32)

        @pl.when(decoder)
        def _():
            for start, size in spans(width, 256):
                columns = pl.ds(start, size)
                total[:, columns] = jnp.dot(
                    rows_in[tick], skip_ref[:width, columns], preferred_element_type=jnp.float32
                ) + jnp.dot(
                    queue_in[tick], skip_ref[width:, columns], preferred_element_type=jnp.float32
                )

        merged = total[...]
        center = jnp.mean(merged, axis=1, keepdims=True)
        spread = jnp.mean(jnp.square(merged - center), axis=1, keepdims=True)
        normed[...] = ((merged - center) * lax.rsqrt(spread + epsilon) * gain_ref[...]).astype(
            jnp.bfloat16
        )

        if tick == 0:
            load_up.wait()

        for start, size in spans(hidden_width, 512):
            columns = pl.ds(start, size)
            hidden[:, columns] = jax.nn.gelu(
                jnp.dot(normed[...], up_ref[:, columns], preferred_element_type=jnp.float32),
                approximate=True,
            ).astype(jnp.bfloat16)

        if tick == 0:
            load_down.wait()

        for start, size in spans(width, 256):
            columns = pl.ds(start, size)
            outputs[tick, :, columns] = (
                total[:, columns]
                + jnp.dot(hidden[...], down_ref[:, columns], preferred_element_type=jnp.float32)
            ).astype(jnp.bfloat16)

        if tick < TICKS - 1:

            @pl.when(me != half - 1)
            def _():
                rows_copy(tick).start()

            if tick == 0:

                @pl.when(far)
                def _():
                    queue_copy(0).start()

            now = encoder if tick < TICKS - 2 else jnp.logical_and(encoder, jnp.logical_not(holds))

            @pl.when(now)
            def _():
                queue_copy(tick + 1).start()
        else:

            @pl.when(me != leader)
            def _():
                rows_copy(tick).start()

            @pl.when(me == leader)
            def _():
                relay_copy(0).start()
                direct_copy.start()

    @pl.when(encoder)
    def _():
        next_queue_ref[0] = outputs[TICKS - 1]

    @pl.when(me == leader)
    def _():
        queue_copy(TICKS - 1).wait_send()
        for peer in holders:
            pl.semaphore_signal(hold_sem, inc=1, device_id={"section": peer}, device_id_type=MESH)

    @pl.when(holds)
    def _():
        pl.semaphore_wait(hold_sem, 1)
        queue_copy(TICKS - 1).start()

    @pl.when(me == helper)
    def _():
        relay_copy(0).wait_recv()
        relay_copy(1).start()

    @pl.when(me != half)
    def _():
        rows_copy(TICKS - 1).wait_recv()

    @pl.when(me == half)
    def _():
        direct_copy.wait_recv()
        relay_copy(1).wait_recv()

    @pl.when(me > half)
    def _():
        queue_copy(TICKS - 1).wait_recv()

    for tick in range(TICKS):
        unsent = encoder if tick < TICKS - 1 else jnp.logical_and(encoder, me != leader)

        @pl.when(unsent)
        def _():
            queue_copy(tick).wait_send()

        if tick < TICKS - 1:

            @pl.when(me != half - 1)
            def _():
                rows_copy(tick).wait_send()
        else:

            @pl.when(me != leader)
            def _():
                rows_copy(tick).wait_send()

            @pl.when(me == leader)
            def _():
                relay_copy(0).wait_send()
                direct_copy.wait_send()

    @pl.when(me == helper)
    def _():
        relay_copy(1).wait_send()


def local(latent_rows, skip_queue, norm_gain, skip_weight, up_weight, down_weight):
    sections = lax.axis_size("section")
    _, row_count, width = latent_rows.shape
    hidden_width = up_weight.shape[2]
    shape = jax.ShapeDtypeStruct(latent_rows.shape, jnp.bfloat16)
    in_hbm = pl.BlockSpec(memory_space=pltpu.HBM)
    in_vmem = pl.BlockSpec(memory_space=pltpu.VMEM)
    return pl.pallas_call(
        functools.partial(kernel, sections),
        out_shape=(shape, shape),
        in_specs=[in_hbm, in_hbm, in_vmem, in_hbm, in_hbm, in_hbm],
        out_specs=(in_vmem, in_vmem),
        scratch_shapes=[
            pltpu.VMEM((2 * width, width), jnp.bfloat16),
            pltpu.VMEM((width, hidden_width), jnp.bfloat16),
            pltpu.VMEM((hidden_width, width), jnp.bfloat16),
            pltpu.VMEM((TICKS, row_count, width), jnp.bfloat16),
            pltpu.VMEM((TICKS, row_count, width), jnp.bfloat16),
            pltpu.VMEM((TICKS, row_count, width), jnp.bfloat16),
            pltpu.VMEM((row_count, width), jnp.float32),
            pltpu.VMEM((row_count, width), jnp.bfloat16),
            pltpu.VMEM((row_count, hidden_width), jnp.bfloat16),
            pltpu.SemaphoreType.DMA((5,)),
            pltpu.SemaphoreType.DMA((TICKS,)),
            pltpu.SemaphoreType.DMA((TICKS,)),
            pltpu.SemaphoreType.DMA((TICKS,)),
            pltpu.SemaphoreType.DMA((TICKS,)),
            pltpu.SemaphoreType.REGULAR,
            pltpu.VMEM((row_count // 2, width), jnp.bfloat16),
            pltpu.SemaphoreType.DMA,
            pltpu.SemaphoreType.DMA,
        ],
        compiler_params=pltpu.CompilerParams(
            collective_id=0, has_side_effects=True, vmem_limit_bytes=52 << 20
        ),
    )(latent_rows, skip_queue, norm_gain, skip_weight, up_weight, down_weight)


def solution(mesh):
    return jax.shard_map(
        local,
        mesh=mesh,
        in_specs=(
            P(("groups", "section"), None, None),
            P(("groups", "section"), None, None),
            P("section", None),
            P("section", None, None),
            P("section", None, None),
            P("section", None, None),
        ),
        out_specs=(P(("groups", "section"), None, None), P(("groups", "section"), None, None)),
        check_vma=False,
    )
```

```python
import functools

import jax
import jax.numpy as jnp
from jax import lax
from jax.experimental import pallas as pl
from jax.experimental.pallas import tpu as pltpu
from jax.sharding import PartitionSpec as P

TICKS = 3


epsilon = 1e-06

MESH = pl.DeviceIdType.MESH


def spans(extent, step):
    return [(start, min(step, extent - start)) for start in range(0, extent, step)]


def kernel(
    sections,
    rows_hbm,
    queue_hbm,
    gain_hbm,
    skip_hbm,
    up_hbm,
    down_hbm,
    next_rows_ref,
    next_queue_ref,
    gain_ref,
    skip_ref,
    up_ref,
    down_ref,
    rows_in,
    queue_in,
    outputs,
    total,
    normed,
    hidden,
    load_sem,
    queue_send,
    queue_recv,
    rows_send,
    rows_recv,
    hold_sem,
    relay,
    relay_send,
    relay_recv,
):
    me = lax.axis_index("section")
    half = sections // 2
    right = lax.rem(me + 1, sections)
    left = lax.rem(me + sections - 1, sections)
    mirror = sections - 1 - me
    encoder = me < half
    decoder = me >= half
    far = jnp.logical_and(me < half // 2, lax.rem(me, 2) == 1)
    near = jnp.logical_and(encoder, jnp.logical_not(far))
    row_count, width = rows_hbm.shape[1:]
    hidden_width = up_ref.shape[1]

    load_up = pltpu.make_async_copy(up_hbm.at[0], up_ref, load_sem.at[0])
    load_down = pltpu.make_async_copy(down_hbm.at[0], down_ref, load_sem.at[1])
    load_rows = pltpu.make_async_copy(rows_hbm.at[0], rows_in.at[0], load_sem.at[2])
    load_skip = pltpu.make_async_copy(skip_hbm.at[0], skip_ref, load_sem.at[3])
    load_queue = pltpu.make_async_copy(queue_hbm.at[0], queue_in.at[0], load_sem.at[4])
    load_gain = pltpu.make_async_copy(gain_hbm, gain_ref, load_sem.at[5])

    leader = half - 1
    holders = [s for s in range(half - 1) if (s // 2 - leader // 2) % 2 == 0 or s < half // 2]
    shares = jnp.logical_or(lax.rem(me // 2 + leader // 2, 2) == 0, me < half // 2)
    holds = jnp.logical_and(me < leader, shares)

    helper = leader - 2
    relayed = relay.shape[0]
    first, rest = pl.ds(0, relayed), pl.ds(relayed, row_count - relayed)

    def relay_copy(hop):
        return pltpu.make_async_remote_copy(
            src_ref=relay if hop else outputs.at[TICKS - 1, first],
            dst_ref=next_rows_ref.at[0, first] if hop else relay,
            send_sem=relay_send,
            recv_sem=relay_recv,
            device_id={"section": half if hop else helper},
            device_id_type=MESH,
        )

    direct_copy = pltpu.make_async_remote_copy(
        src_ref=outputs.at[TICKS - 1, rest],
        dst_ref=next_rows_ref.at[0, rest],
        send_sem=rows_send.at[TICKS - 1],
        recv_sem=rows_recv.at[TICKS - 1],
        device_id={"section": half},
        device_id_type=MESH,
    )

    def queue_copy(tick):
        source = queue_hbm.at[0] if tick == 0 else outputs.at[tick - 1]
        return pltpu.make_async_remote_copy(
            src_ref=source,
            dst_ref=next_queue_ref.at[0] if tick == TICKS - 1 else queue_in.at[tick + 1],
            send_sem=queue_send.at[tick],
            recv_sem=queue_recv.at[tick],
            device_id={"section": mirror},
            device_id_type=MESH,
        )

    def rows_copy(tick):
        return pltpu.make_async_remote_copy(
            src_ref=outputs.at[tick],
            dst_ref=next_rows_ref.at[0] if tick == TICKS - 1 else rows_in.at[tick + 1],
            send_sem=rows_send.at[tick],
            recv_sem=rows_recv.at[tick],
            device_id={"section": right},
            device_id_type=MESH,
        )

    barrier = pltpu.get_barrier_semaphore()
    pl.semaphore_signal(barrier, inc=1, device_id={"section": left}, device_id_type=MESH)

    @pl.when(decoder)
    def _():
        pl.semaphore_signal(barrier, inc=1, device_id={"section": mirror}, device_id_type=MESH)

    @pl.when(holds)
    def _():
        pl.semaphore_signal(barrier, inc=1, device_id={"section": leader}, device_id_type=MESH)

    @pl.when(me == half)
    def _():
        pl.semaphore_signal(barrier, inc=1, device_id={"section": helper}, device_id_type=MESH)

    @pl.when(me == helper)
    def _():
        pl.semaphore_signal(barrier, inc=1, device_id={"section": leader}, device_id_type=MESH)
        pl.semaphore_wait(barrier, 3)

    @pl.when(me == leader)
    def _():
        pl.semaphore_wait(barrier, 3 + len(holders))

    @pl.when(jnp.logical_and(encoder, jnp.logical_and(me != leader, me != helper)))
    def _():
        pl.semaphore_wait(barrier, 2)

    @pl.when(decoder)
    def _():
        pl.semaphore_wait(barrier, 1)

    @pl.when(near)
    def _():
        queue_copy(0).start()

    load_rows.start()
    load_gain.start()
    load_up.start()
    load_down.start()

    @pl.when(decoder)
    def _():
        load_queue.start()
        load_skip.start()

    for tick in range(TICKS):
        if tick == 0:
            load_rows.wait()
            load_gain.wait()

            @pl.when(decoder)
            def _():
                load_queue.wait()
                load_skip.wait()
        else:
            @pl.when(me != half)
            def _():
                rows_copy(tick - 1).wait_recv()

            if tick == 1:

                @pl.when(decoder)
                def _():
                    queue_copy(0).wait_recv()
            else:

                @pl.when(me > half)
                def _():
                    queue_copy(tick - 1).wait_recv()

            @pl.when(me == half)
            def _():
                queue_copy(tick).wait_recv()
                rows_in[tick] = next_queue_ref[0] if tick == TICKS - 1 else queue_in[tick + 1]

        @pl.when(encoder)
        def _():
            total[...] = rows_in[tick].astype(jnp.float32)

        @pl.when(decoder)
        def _():
            for start, size in spans(width, 256):
                columns = pl.ds(start, size)
                total[:, columns] = jnp.dot(
                    rows_in[tick], skip_ref[:width, columns], preferred_element_type=jnp.float32
                ) + jnp.dot(
                    queue_in[tick], skip_ref[width:, columns], preferred_element_type=jnp.float32
                )

        merged = total[...]
        center = jnp.mean(merged, axis=1, keepdims=True)
        spread = jnp.mean(jnp.square(merged - center), axis=1, keepdims=True)
        normed[...] = ((merged - center) * lax.rsqrt(spread + epsilon) * gain_ref[...]).astype(
            jnp.bfloat16
        )

        if tick == 0:
            load_up.wait()

        for start, size in spans(hidden_width, 512):
            columns = pl.ds(start, size)
            hidden[:, columns] = jax.nn.gelu(
                jnp.dot(normed[...], up_ref[:, columns], preferred_element_type=jnp.float32),
                approximate=True,
            ).astype(jnp.bfloat16)

        if tick == 0:
            load_down.wait()

        for start, size in spans(width, 256):
            columns = pl.ds(start, size)
            outputs[tick, :, columns] = (
                total[:, columns]
                + jnp.dot(hidden[...], down_ref[:, columns], preferred_element_type=jnp.float32)
            ).astype(jnp.bfloat16)

        if tick < TICKS - 1:

            @pl.when(me != half - 1)
            def _():
                rows_copy(tick).start()

            if tick == 0:

                @pl.when(far)
                def _():
                    queue_copy(0).start()

            now = encoder if tick < TICKS - 2 else jnp.logical_and(encoder, jnp.logical_not(holds))

            @pl.when(now)
            def _():
                queue_copy(tick + 1).start()
        else:

            @pl.when(me != leader)
            def _():
                rows_copy(tick).start()

            @pl.when(me == leader)
            def _():
                relay_copy(0).start()
                direct_copy.start()

    @pl.when(encoder)
    def _():
        next_queue_ref[0] = outputs[TICKS - 1]

    @pl.when(me == leader)
    def _():
        queue_copy(TICKS - 1).wait_send()
        for peer in holders:
            pl.semaphore_signal(hold_sem, inc=1, device_id={"section": peer}, device_id_type=MESH)

    @pl.when(holds)
    def _():
        pl.semaphore_wait(hold_sem, 1)
        queue_copy(TICKS - 1).start()

    @pl.when(me == helper)
    def _():
        relay_copy(0).wait_recv()
        relay_copy(1).start()

    @pl.when(me != half)
    def _():
        rows_copy(TICKS - 1).wait_recv()

    @pl.when(me == half)
    def _():
        direct_copy.wait_recv()
        relay_copy(1).wait_recv()

    @pl.when(me > half)
    def _():
        queue_copy(TICKS - 1).wait_recv()

    for tick in range(TICKS):
        unsent = encoder if tick < TICKS - 1 else jnp.logical_and(encoder, me != leader)

        @pl.when(unsent)
        def _():
            queue_copy(tick).wait_send()

        if tick < TICKS - 1:

            @pl.when(me != half - 1)
            def _():
                rows_copy(tick).wait_send()
        else:

            @pl.when(me != leader)
            def _():
                rows_copy(tick).wait_send()

            @pl.when(me == leader)
            def _():
                relay_copy(0).wait_send()
                direct_copy.wait_send()

    @pl.when(me == helper)
    def _():
        relay_copy(1).wait_send()


def store(rows_ref, queue_ref, rows_hbm, queue_hbm, sem):
    copies = [
        pltpu.make_async_copy(rows_ref, rows_hbm, sem.at[0]),
        pltpu.make_async_copy(queue_ref, queue_hbm, sem.at[1]),
    ]
    for copy in copies:
        copy.start()
    for copy in copies:
        copy.wait()


def local(latent_rows, skip_queue, norm_gain, skip_weight, up_weight, down_weight):
    sections = lax.axis_size("section")
    _, row_count, width = latent_rows.shape
    hidden_width = up_weight.shape[2]
    shape = jax.ShapeDtypeStruct(latent_rows.shape, jnp.bfloat16)
    relayed = row_count * 7 // 256 * 16
    in_hbm = pl.BlockSpec(memory_space=pltpu.HBM)
    in_vmem = pl.BlockSpec(memory_space=pltpu.VMEM)
    results = pl.pallas_call(
        functools.partial(kernel, sections),
        out_shape=(shape, shape),
        in_specs=[in_hbm] * 6,
        out_specs=(in_vmem, in_vmem),
        scratch_shapes=[
            pltpu.VMEM((1, width), jnp.float32),
            pltpu.VMEM((2 * width, width), jnp.bfloat16),
            pltpu.VMEM((width, hidden_width), jnp.bfloat16),
            pltpu.VMEM((hidden_width, width), jnp.bfloat16),
            pltpu.VMEM((TICKS, row_count, width), jnp.bfloat16),
            pltpu.VMEM((TICKS, row_count, width), jnp.bfloat16),
            pltpu.VMEM((TICKS, row_count, width), jnp.bfloat16),
            pltpu.VMEM((row_count, width), jnp.float32),
            pltpu.VMEM((row_count, width), jnp.bfloat16),
            pltpu.VMEM((row_count, hidden_width), jnp.bfloat16),
            pltpu.SemaphoreType.DMA((6,)),
            pltpu.SemaphoreType.DMA((TICKS,)),
            pltpu.SemaphoreType.DMA((TICKS,)),
            pltpu.SemaphoreType.DMA((TICKS,)),
            pltpu.SemaphoreType.DMA((TICKS,)),
            pltpu.SemaphoreType.REGULAR,
            pltpu.VMEM((relayed, width), jnp.bfloat16),
            pltpu.SemaphoreType.DMA,
            pltpu.SemaphoreType.DMA,
        ],
        compiler_params=pltpu.CompilerParams(
            collective_id=0, has_side_effects=True, vmem_limit_bytes=52 << 20
        ),
    )(latent_rows, skip_queue, pltpu.with_memory_space_constraint(norm_gain, pltpu.HBM), skip_weight, up_weight, down_weight)
    return pl.pallas_call(
        store,
        out_shape=(shape, shape),
        in_specs=[pl.BlockSpec(memory_space=pl.ANY)] * 2,
        out_specs=(in_hbm, in_hbm),
        scratch_shapes=[pltpu.SemaphoreType.DMA((2,))],
        compiler_params=pltpu.CompilerParams(vmem_limit_bytes=1 << 20),
    )(*results)


def solution(mesh):
    return jax.shard_map(
        local,
        mesh=mesh,
        in_specs=(
            P(("groups", "section"), None, None),
            P(("groups", "section"), None, None),
            P("section", None),
            P("section", None, None),
            P("section", None, None),
            P("section", None, None),
        ),
        out_specs=(P(("groups", "section"), None, None), P(("groups", "section"), None, None)),
        check_vma=False,
    )
```

```python
import functools

import jax
import jax.numpy as jnp
from jax import lax
from jax.experimental import pallas as pl
from jax.experimental.pallas import tpu as pltpu
from jax.sharding import PartitionSpec as P

TICKS = 3


epsilon = 1e-06

MESH = pl.DeviceIdType.MESH


def spans(extent, step):
    return [(start, min(step, extent - start)) for start in range(0, extent, step)]


def kernel(
    sections,
    rows_hbm,
    queue_hbm,
    gain_hbm,
    skip_hbm,
    up_hbm,
    down_hbm,
    next_rows_ref,
    next_queue_ref,
    gain_ref,
    skip_ref,
    up_ref,
    down_ref,
    rows_in,
    queue_in,
    outputs,
    total,
    normed,
    hidden,
    load_sem,
    queue_send,
    queue_recv,
    rows_send,
    rows_recv,
    hold_sem,
    relay,
    relay_send,
    relay_recv,
):
    me = lax.axis_index("section")
    half = sections // 2
    right = lax.rem(me + 1, sections)
    left = lax.rem(me + sections - 1, sections)
    mirror = sections - 1 - me
    encoder = me < half
    decoder = me >= half
    far = jnp.logical_and(me < half // 2, lax.rem(me, 2) == 1)
    near = jnp.logical_and(encoder, jnp.logical_not(far))
    row_count, width = rows_hbm.shape[1:]
    hidden_width = up_ref.shape[1]

    load_up = pltpu.make_async_copy(up_hbm.at[0], up_ref, load_sem.at[0])
    load_down = pltpu.make_async_copy(down_hbm.at[0], down_ref, load_sem.at[1])
    load_rows = pltpu.make_async_copy(rows_hbm.at[0], rows_in.at[0], load_sem.at[2])
    load_skip = pltpu.make_async_copy(skip_hbm.at[0], skip_ref, load_sem.at[3])
    load_queue = pltpu.make_async_copy(queue_hbm.at[0], queue_in.at[0], load_sem.at[4])
    load_gain = pltpu.make_async_copy(gain_hbm, gain_ref, load_sem.at[5])

    leader = half - 1
    holders = range(half // 2)
    holds = me < half // 2

    helper = leader - 2
    relayed = relay.shape[0]
    first, rest = pl.ds(0, relayed), pl.ds(relayed, row_count - relayed)

    def relay_copy(hop):
        return pltpu.make_async_remote_copy(
            src_ref=relay if hop else outputs.at[TICKS - 1, first],
            dst_ref=next_rows_ref.at[0, first] if hop else relay,
            send_sem=relay_send,
            recv_sem=relay_recv,
            device_id={"section": half if hop else helper},
            device_id_type=MESH,
        )

    direct_copy = pltpu.make_async_remote_copy(
        src_ref=outputs.at[TICKS - 1, rest],
        dst_ref=next_rows_ref.at[0, rest],
        send_sem=rows_send.at[TICKS - 1],
        recv_sem=rows_recv.at[TICKS - 1],
        device_id={"section": half},
        device_id_type=MESH,
    )

    def queue_copy(tick):
        source = queue_hbm.at[0] if tick == 0 else outputs.at[tick - 1]
        return pltpu.make_async_remote_copy(
            src_ref=source,
            dst_ref=next_queue_ref.at[0] if tick == TICKS - 1 else queue_in.at[tick + 1],
            send_sem=queue_send.at[tick],
            recv_sem=queue_recv.at[tick],
            device_id={"section": mirror},
            device_id_type=MESH,
        )

    def rows_copy(tick):
        return pltpu.make_async_remote_copy(
            src_ref=outputs.at[tick],
            dst_ref=next_rows_ref.at[0] if tick == TICKS - 1 else rows_in.at[tick + 1],
            send_sem=rows_send.at[tick],
            recv_sem=rows_recv.at[tick],
            device_id={"section": right},
            device_id_type=MESH,
        )

    barrier = pltpu.get_barrier_semaphore()

    @pl.when(decoder)
    def _():
        pl.semaphore_signal(barrier, inc=1, device_id={"section": mirror}, device_id_type=MESH)

    pl.semaphore_signal(barrier, inc=1, device_id={"section": left}, device_id_type=MESH)

    @pl.when(holds)
    def _():
        pl.semaphore_signal(barrier, inc=1, device_id={"section": leader}, device_id_type=MESH)

    @pl.when(me == half)
    def _():
        pl.semaphore_signal(barrier, inc=1, device_id={"section": helper}, device_id_type=MESH)

    @pl.when(me == helper)
    def _():
        pl.semaphore_signal(barrier, inc=1, device_id={"section": leader}, device_id_type=MESH)
        pl.semaphore_wait(barrier, 3)

    @pl.when(me == leader)
    def _():
        pl.semaphore_wait(barrier, 3 + len(holders))

    @pl.when(jnp.logical_and(encoder, jnp.logical_and(me != leader, me != helper)))
    def _():
        pl.semaphore_wait(barrier, 2)

    @pl.when(decoder)
    def _():
        pl.semaphore_wait(barrier, 1)

    @pl.when(near)
    def _():
        queue_copy(0).start()

    load_rows.start()
    load_gain.start()
    load_up.start()
    load_down.start()

    @pl.when(decoder)
    def _():
        load_queue.start()
        load_skip.start()

    for tick in range(TICKS):
        if tick == 0:
            load_rows.wait()
            load_gain.wait()

            @pl.when(decoder)
            def _():
                load_queue.wait()
                load_skip.wait()
        else:
            @pl.when(me != half)
            def _():
                rows_copy(tick - 1).wait_recv()

            if tick == 1:

                @pl.when(decoder)
                def _():
                    queue_copy(0).wait_recv()
            else:

                @pl.when(me > half)
                def _():
                    queue_copy(tick - 1).wait_recv()

            @pl.when(me == half)
            def _():
                queue_copy(tick).wait_recv()
                rows_in[tick] = next_queue_ref[0] if tick == TICKS - 1 else queue_in[tick + 1]

        @pl.when(encoder)
        def _():
            total[...] = rows_in[tick].astype(jnp.float32)

        @pl.when(decoder)
        def _():
            for start, size in spans(width, 256):
                columns = pl.ds(start, size)
                total[:, columns] = jnp.dot(
                    rows_in[tick], skip_ref[:width, columns], preferred_element_type=jnp.float32
                ) + jnp.dot(
                    queue_in[tick], skip_ref[width:, columns], preferred_element_type=jnp.float32
                )

        merged = total[...]
        center = jnp.mean(merged, axis=1, keepdims=True)
        spread = jnp.mean(jnp.square(merged - center), axis=1, keepdims=True)
        normed[...] = ((merged - center) * lax.rsqrt(spread + epsilon) * gain_ref[...]).astype(
            jnp.bfloat16
        )

        if tick == 0:
            load_up.wait()

        for start, size in spans(hidden_width, 512):
            columns = pl.ds(start, size)
            hidden[:, columns] = jax.nn.gelu(
                jnp.dot(normed[...], up_ref[:, columns], preferred_element_type=jnp.float32),
                approximate=True,
            ).astype(jnp.bfloat16)

        if tick == 0:
            load_down.wait()

        for start, size in spans(width, 256):
            columns = pl.ds(start, size)
            outputs[tick, :, columns] = (
                total[:, columns]
                + jnp.dot(hidden[...], down_ref[:, columns], preferred_element_type=jnp.float32)
            ).astype(jnp.bfloat16)

        if tick < TICKS - 1:

            @pl.when(me != half - 1)
            def _():
                rows_copy(tick).start()

            if tick == 0:

                @pl.when(far)
                def _():
                    queue_copy(0).start()

            now = encoder if tick < TICKS - 2 else jnp.logical_and(encoder, jnp.logical_not(holds))

            @pl.when(now)
            def _():
                queue_copy(tick + 1).start()
        else:

            @pl.when(me != leader)
            def _():
                rows_copy(tick).start()

            @pl.when(me == leader)
            def _():
                relay_copy(0).start()
                direct_copy.start()

    @pl.when(encoder)
    def _():
        next_queue_ref[0] = outputs[TICKS - 1]

    @pl.when(me == leader)
    def _():
        queue_copy(TICKS - 1).wait_send()
        for peer in holders:
            pl.semaphore_signal(hold_sem, inc=1, device_id={"section": peer}, device_id_type=MESH)

    @pl.when(holds)
    def _():
        pl.semaphore_wait(hold_sem, 1)
        queue_copy(TICKS - 1).start()

    @pl.when(me == helper)
    def _():
        relay_copy(0).wait_recv()
        relay_copy(1).start()

    @pl.when(me != half)
    def _():
        rows_copy(TICKS - 1).wait_recv()

    @pl.when(me == half)
    def _():
        direct_copy.wait_recv()
        relay_copy(1).wait_recv()

    @pl.when(me > half)
    def _():
        queue_copy(TICKS - 1).wait_recv()

    for tick in range(TICKS):
        unsent = encoder if tick < TICKS - 1 else jnp.logical_and(encoder, me != leader)

        @pl.when(unsent)
        def _():
            queue_copy(tick).wait_send()

        if tick < TICKS - 1:

            @pl.when(me != half - 1)
            def _():
                rows_copy(tick).wait_send()
        else:

            @pl.when(me != leader)
            def _():
                rows_copy(tick).wait_send()

            @pl.when(me == leader)
            def _():
                relay_copy(0).wait_send()
                direct_copy.wait_send()

    @pl.when(me == helper)
    def _():
        relay_copy(1).wait_send()


def store(rows_ref, queue_ref, rows_hbm, queue_hbm, sem):
    copies = [
        pltpu.make_async_copy(rows_ref, rows_hbm, sem.at[0]),
        pltpu.make_async_copy(queue_ref, queue_hbm, sem.at[1]),
    ]
    for copy in copies:
        copy.start()
    for copy in copies:
        copy.wait()


def local(latent_rows, skip_queue, norm_gain, skip_weight, up_weight, down_weight):
    sections = lax.axis_size("section")
    _, row_count, width = latent_rows.shape
    hidden_width = up_weight.shape[2]
    shape = jax.ShapeDtypeStruct(latent_rows.shape, jnp.bfloat16)
    relayed = row_count // 32 * 16
    in_hbm = pl.BlockSpec(memory_space=pltpu.HBM)
    in_vmem = pl.BlockSpec(memory_space=pltpu.VMEM)
    results = pl.pallas_call(
        functools.partial(kernel, sections),
        out_shape=(shape, shape),
        in_specs=[in_hbm] * 6,
        out_specs=(in_vmem, in_vmem),
        scratch_shapes=[
            pltpu.VMEM((1, width), jnp.float32),
            pltpu.VMEM((2 * width, width), jnp.bfloat16),
            pltpu.VMEM((width, hidden_width), jnp.bfloat16),
            pltpu.VMEM((hidden_width, width), jnp.bfloat16),
            pltpu.VMEM((TICKS, row_count, width), jnp.bfloat16),
            pltpu.VMEM((TICKS, row_count, width), jnp.bfloat16),
            pltpu.VMEM((TICKS, row_count, width), jnp.bfloat16),
            pltpu.VMEM((row_count, width), jnp.float32),
            pltpu.VMEM((row_count, width), jnp.bfloat16),
            pltpu.VMEM((row_count, hidden_width), jnp.bfloat16),
            pltpu.SemaphoreType.DMA((6,)),
            pltpu.SemaphoreType.DMA((TICKS,)),
            pltpu.SemaphoreType.DMA((TICKS,)),
            pltpu.SemaphoreType.DMA((TICKS,)),
            pltpu.SemaphoreType.DMA((TICKS,)),
            pltpu.SemaphoreType.REGULAR,
            pltpu.VMEM((relayed, width), jnp.bfloat16),
            pltpu.SemaphoreType.DMA,
            pltpu.SemaphoreType.DMA,
        ],
        compiler_params=pltpu.CompilerParams(
            collective_id=0, has_side_effects=True, vmem_limit_bytes=52 << 20
        ),
    )(latent_rows, skip_queue, pltpu.with_memory_space_constraint(norm_gain, pltpu.HBM), skip_weight, up_weight, down_weight)
    return pl.pallas_call(
        store,
        out_shape=(shape, shape),
        in_specs=[pl.BlockSpec(memory_space=pl.ANY)] * 2,
        out_specs=(in_hbm, in_hbm),
        scratch_shapes=[pltpu.SemaphoreType.DMA((2,))],
        compiler_params=pltpu.CompilerParams(vmem_limit_bytes=1 << 20),
    )(*results)


def solution(mesh):
    return jax.shard_map(
        local,
        mesh=mesh,
        in_specs=(
            P(("groups", "section"), None, None),
            P(("groups", "section"), None, None),
            P("section", None),
            P("section", None, None),
            P("section", None, None),
            P("section", None, None),
        ),
        out_specs=(P(("groups", "section"), None, None), P(("groups", "section"), None, None)),
        check_vma=False,
    )
```

```python
import functools

import jax
import jax.numpy as jnp
from jax import lax
from jax.experimental import pallas as pl
from jax.experimental.pallas import tpu as pltpu
from jax.sharding import PartitionSpec as P

TICKS = 3


epsilon = 1e-06

MESH = pl.DeviceIdType.MESH


def spans(extent, step):
    return [(start, min(step, extent - start)) for start in range(0, extent, step)]


def kernel(
    sections,
    rows_hbm,
    queue_hbm,
    gain_hbm,
    skip_hbm,
    up_hbm,
    down_hbm,
    next_rows_ref,
    next_queue_ref,
    gain_ref,
    skip_ref,
    up_ref,
    down_ref,
    rows_in,
    queue_in,
    outputs,
    total,
    normed,
    hidden,
    load_sem,
    queue_send,
    queue_recv,
    rows_send,
    rows_recv,
    hold_sem,
    relay,
    relay_send,
    relay_recv,
):
    me = lax.axis_index("section")
    half = sections // 2
    right = lax.rem(me + 1, sections)
    left = lax.rem(me + sections - 1, sections)
    mirror = sections - 1 - me
    encoder = me < half
    decoder = me >= half
    far = jnp.logical_and(me < half // 2, lax.rem(me, 2) == 1)
    near = jnp.logical_and(encoder, jnp.logical_not(far))
    row_count, width = rows_hbm.shape[1:]
    hidden_width = up_ref.shape[1]

    load_up = pltpu.make_async_copy(up_hbm.at[0], up_ref, load_sem.at[0])
    load_down = pltpu.make_async_copy(down_hbm.at[0], down_ref, load_sem.at[1])
    load_rows = pltpu.make_async_copy(rows_hbm.at[0], rows_in.at[0], load_sem.at[2])
    load_skip = pltpu.make_async_copy(skip_hbm.at[0], skip_ref, load_sem.at[3])
    load_queue = pltpu.make_async_copy(queue_hbm.at[0], queue_in.at[0], load_sem.at[4])
    load_gain = pltpu.make_async_copy(gain_hbm, gain_ref, load_sem.at[5])

    leader = half - 1
    holders = range(half // 2)
    holds = me < half // 2

    helper = leader - 2
    relayed = relay.shape[0]
    first, rest = pl.ds(0, relayed), pl.ds(relayed, row_count - relayed)

    def relay_copy(hop):
        return pltpu.make_async_remote_copy(
            src_ref=relay if hop else outputs.at[TICKS - 1, first],
            dst_ref=next_rows_ref.at[0, first] if hop else relay,
            send_sem=relay_send,
            recv_sem=relay_recv,
            device_id={"section": half if hop else helper},
            device_id_type=MESH,
        )

    direct_copy = pltpu.make_async_remote_copy(
        src_ref=outputs.at[TICKS - 1, rest],
        dst_ref=next_rows_ref.at[0, rest],
        send_sem=rows_send.at[TICKS - 1],
        recv_sem=rows_recv.at[TICKS - 1],
        device_id={"section": half},
        device_id_type=MESH,
    )

    ahead, via = half - 4, half + 1
    target = sections - 1 - ahead
    early = row_count // 64 * 16
    soon, later = pl.ds(0, early), pl.ds(early, row_count - early)

    def early_copy(hop):
        return pltpu.make_async_remote_copy(
            src_ref=relay.at[soon] if hop else queue_hbm.at[0, soon],
            dst_ref=queue_in.at[1, soon] if hop else relay.at[soon],
            send_sem=relay_send,
            recv_sem=relay_recv,
            device_id={"section": target if hop else via},
            device_id_type=MESH,
        )

    late_copy = pltpu.make_async_remote_copy(
        src_ref=queue_hbm.at[0, later],
        dst_ref=queue_in.at[1, later],
        send_sem=queue_send.at[0],
        recv_sem=queue_recv.at[0],
        device_id={"section": target},
        device_id_type=MESH,
    )

    def queue_copy(tick):
        source = queue_hbm.at[0] if tick == 0 else outputs.at[tick - 1]
        return pltpu.make_async_remote_copy(
            src_ref=source,
            dst_ref=next_queue_ref.at[0] if tick == TICKS - 1 else queue_in.at[tick + 1],
            send_sem=queue_send.at[tick],
            recv_sem=queue_recv.at[tick],
            device_id={"section": mirror},
            device_id_type=MESH,
        )

    def rows_copy(tick):
        return pltpu.make_async_remote_copy(
            src_ref=outputs.at[tick],
            dst_ref=next_rows_ref.at[0] if tick == TICKS - 1 else rows_in.at[tick + 1],
            send_sem=rows_send.at[tick],
            recv_sem=rows_recv.at[tick],
            device_id={"section": right},
            device_id_type=MESH,
        )

    barrier = pltpu.get_barrier_semaphore()

    def greet(sem, peer):
        pl.semaphore_signal(sem, inc=1, device_id={"section": peer}, device_id_type=MESH)

    @pl.when(me == via)
    def _():
        greet(barrier, ahead)

    @pl.when(jnp.logical_and(decoder, me != target))
    def _():
        greet(barrier, mirror)

    @pl.when(me == target)
    def _():
        greet(barrier, via)

    @pl.when(me != helper)
    def _():
        greet(barrier, left)

    @pl.when(me == ahead)
    def _():
        greet(barrier, target)
        greet(barrier, helper)

    @pl.when(jnp.logical_or(holds, me == helper))
    def _():
        greet(barrier, leader)

    @pl.when(me == half)
    def _():
        greet(barrier, helper)

    @pl.when(me == ahead)
    def _():
        pl.semaphore_wait(barrier, 1)
        early_copy(0).start()

    @pl.when(me == helper)
    def _():
        pl.semaphore_wait(barrier, 4)
        greet(hold_sem, ahead)

    @pl.when(me == leader)
    def _():
        pl.semaphore_wait(barrier, 3 + len(holders))

    @pl.when(
        jnp.logical_and(
            jnp.logical_and(encoder, me != ahead), jnp.logical_and(me != helper, me != leader)
        )
    )
    def _():
        pl.semaphore_wait(barrier, 2)

    @pl.when(me == target)
    def _():
        pl.semaphore_wait(barrier, 2)
        greet(hold_sem, ahead)

    @pl.when(me == via)
    def _():
        pl.semaphore_wait(barrier, 2)

    @pl.when(jnp.logical_and(decoder, jnp.logical_and(me != target, me != via)))
    def _():
        pl.semaphore_wait(barrier, 1)

    @pl.when(jnp.logical_and(near, me != ahead))
    def _():
        queue_copy(0).start()

    load_rows.start()
    load_gain.start()
    load_up.start()
    load_down.start()

    @pl.when(decoder)
    def _():
        load_queue.start()
        load_skip.start()

    @pl.when(me == ahead)
    def _():
        pl.semaphore_wait(hold_sem, 2)
        late_copy.start()

    @pl.when(me == via)
    def _():
        early_copy(0).wait_recv()
        early_copy(1).start()

    for tick in range(TICKS):
        if tick == 0:
            load_rows.wait()
            load_gain.wait()

            @pl.when(decoder)
            def _():
                load_queue.wait()
                load_skip.wait()
        else:
            @pl.when(me != half)
            def _():
                rows_copy(tick - 1).wait_recv()

            if tick == 1:

                @pl.when(jnp.logical_and(decoder, me != target))
                def _():
                    queue_copy(0).wait_recv()

                @pl.when(me == target)
                def _():
                    early_copy(1).wait_recv()
                    late_copy.wait_recv()
            else:

                @pl.when(me > half)
                def _():
                    queue_copy(tick - 1).wait_recv()

            @pl.when(me == half)
            def _():
                queue_copy(tick).wait_recv()
                rows_in[tick] = next_queue_ref[0] if tick == TICKS - 1 else queue_in[tick + 1]

        @pl.when(encoder)
        def _():
            total[...] = rows_in[tick].astype(jnp.float32)

        @pl.when(decoder)
        def _():
            for start, size in spans(width, 256):
                columns = pl.ds(start, size)
                total[:, columns] = jnp.dot(
                    rows_in[tick], skip_ref[:width, columns], preferred_element_type=jnp.float32
                ) + jnp.dot(
                    queue_in[tick], skip_ref[width:, columns], preferred_element_type=jnp.float32
                )

        merged = total[...]
        center = jnp.mean(merged, axis=1, keepdims=True)
        spread = jnp.mean(jnp.square(merged - center), axis=1, keepdims=True)
        normed[...] = ((merged - center) * lax.rsqrt(spread + epsilon) * gain_ref[...]).astype(
            jnp.bfloat16
        )

        if tick == 0:
            load_up.wait()

        for start, size in spans(hidden_width, 512):
            columns = pl.ds(start, size)
            hidden[:, columns] = jax.nn.gelu(
                jnp.dot(normed[...], up_ref[:, columns], preferred_element_type=jnp.float32),
                approximate=True,
            ).astype(jnp.bfloat16)

        if tick == 0:
            load_down.wait()

        for start, size in spans(width, 256):
            columns = pl.ds(start, size)
            outputs[tick, :, columns] = (
                total[:, columns]
                + jnp.dot(hidden[...], down_ref[:, columns], preferred_element_type=jnp.float32)
            ).astype(jnp.bfloat16)

        if tick < TICKS - 1:

            @pl.when(me != half - 1)
            def _():
                rows_copy(tick).start()

            if tick == 0:

                @pl.when(far)
                def _():
                    queue_copy(0).start()

            now = encoder if tick < TICKS - 2 else jnp.logical_and(encoder, jnp.logical_not(holds))

            @pl.when(now)
            def _():
                queue_copy(tick + 1).start()
        else:

            @pl.when(me != leader)
            def _():
                rows_copy(tick).start()

            @pl.when(me == leader)
            def _():
                relay_copy(0).start()
                direct_copy.start()

    @pl.when(encoder)
    def _():
        next_queue_ref[0] = outputs[TICKS - 1]

    @pl.when(me == leader)
    def _():
        queue_copy(TICKS - 1).wait_send()
        for peer in holders:
            pl.semaphore_signal(hold_sem, inc=1, device_id={"section": peer}, device_id_type=MESH)

    @pl.when(holds)
    def _():
        pl.semaphore_wait(hold_sem, 1)
        queue_copy(TICKS - 1).start()

    @pl.when(me == helper)
    def _():
        relay_copy(0).wait_recv()
        relay_copy(1).start()

    @pl.when(me != half)
    def _():
        rows_copy(TICKS - 1).wait_recv()

    @pl.when(me == half)
    def _():
        direct_copy.wait_recv()
        relay_copy(1).wait_recv()

    @pl.when(me > half)
    def _():
        queue_copy(TICKS - 1).wait_recv()

    for tick in range(TICKS):
        unsent = encoder
        if tick == 0:
            unsent = jnp.logical_and(encoder, me != ahead)
        elif tick == TICKS - 1:
            unsent = jnp.logical_and(encoder, me != leader)

        @pl.when(unsent)
        def _():
            queue_copy(tick).wait_send()

        if tick < TICKS - 1:

            @pl.when(me != half - 1)
            def _():
                rows_copy(tick).wait_send()
        else:

            @pl.when(me != leader)
            def _():
                rows_copy(tick).wait_send()

            @pl.when(me == leader)
            def _():
                relay_copy(0).wait_send()
                direct_copy.wait_send()

    @pl.when(me == helper)
    def _():
        relay_copy(1).wait_send()

    @pl.when(me == ahead)
    def _():
        early_copy(0).wait_send()
        late_copy.wait_send()

    @pl.when(me == via)
    def _():
        early_copy(1).wait_send()


def store(rows_ref, queue_ref, rows_hbm, queue_hbm, sem):
    copies = [
        pltpu.make_async_copy(rows_ref, rows_hbm, sem.at[0]),
        pltpu.make_async_copy(queue_ref, queue_hbm, sem.at[1]),
    ]
    for copy in copies:
        copy.start()
    for copy in copies:
        copy.wait()


def local(latent_rows, skip_queue, norm_gain, skip_weight, up_weight, down_weight):
    sections = lax.axis_size("section")
    _, row_count, width = latent_rows.shape
    hidden_width = up_weight.shape[2]
    shape = jax.ShapeDtypeStruct(latent_rows.shape, jnp.bfloat16)
    relayed = row_count * 9 // 256 * 16
    in_hbm = pl.BlockSpec(memory_space=pltpu.HBM)
    in_vmem = pl.BlockSpec(memory_space=pltpu.VMEM)
    results = pl.pallas_call(
        functools.partial(kernel, sections),
        out_shape=(shape, shape),
        in_specs=[in_hbm] * 6,
        out_specs=(in_vmem, in_vmem),
        scratch_shapes=[
            pltpu.VMEM((1, width), jnp.float32),
            pltpu.VMEM((2 * width, width), jnp.bfloat16),
            pltpu.VMEM((width, hidden_width), jnp.bfloat16),
            pltpu.VMEM((hidden_width, width), jnp.bfloat16),
            pltpu.VMEM((TICKS, row_count, width), jnp.bfloat16),
            pltpu.VMEM((TICKS, row_count, width), jnp.bfloat16),
            pltpu.VMEM((TICKS, row_count, width), jnp.bfloat16),
            pltpu.VMEM((row_count, width), jnp.float32),
            pltpu.VMEM((row_count, width), jnp.bfloat16),
            pltpu.VMEM((row_count, hidden_width), jnp.bfloat16),
            pltpu.SemaphoreType.DMA((6,)),
            pltpu.SemaphoreType.DMA((TICKS,)),
            pltpu.SemaphoreType.DMA((TICKS,)),
            pltpu.SemaphoreType.DMA((TICKS,)),
            pltpu.SemaphoreType.DMA((TICKS,)),
            pltpu.SemaphoreType.REGULAR,
            pltpu.VMEM((relayed, width), jnp.bfloat16),
            pltpu.SemaphoreType.DMA,
            pltpu.SemaphoreType.DMA,
        ],
        compiler_params=pltpu.CompilerParams(
            collective_id=0, has_side_effects=True, vmem_limit_bytes=52 << 20
        ),
    )(latent_rows, skip_queue, pltpu.with_memory_space_constraint(norm_gain, pltpu.HBM), skip_weight, up_weight, down_weight)
    return pl.pallas_call(
        store,
        out_shape=(shape, shape),
        in_specs=[pl.BlockSpec(memory_space=pl.ANY)] * 2,
        out_specs=(in_hbm, in_hbm),
        scratch_shapes=[pltpu.SemaphoreType.DMA((2,))],
        compiler_params=pltpu.CompilerParams(vmem_limit_bytes=1 << 20),
    )(*results)


def solution(mesh):
    return jax.shard_map(
        local,
        mesh=mesh,
        in_specs=(
            P(("groups", "section"), None, None),
            P(("groups", "section"), None, None),
            P("section", None),
            P("section", None, None),
            P("section", None, None),
            P("section", None, None),
        ),
        out_specs=(P(("groups", "section"), None, None), P(("groups", "section"), None, None)),
        check_vma=False,
    )
```

```python
import functools

import jax
import jax.numpy as jnp
from jax import lax
from jax.experimental import pallas as pl
from jax.experimental.pallas import tpu as pltpu
from jax.sharding import PartitionSpec as P

TICKS = 3


epsilon = 1e-06

MESH = pl.DeviceIdType.MESH


def spans(extent, step):
    return [(start, min(step, extent - start)) for start in range(0, extent, step)]


def kernel(
    sections,
    rows_hbm,
    queue_hbm,
    gain_hbm,
    skip_hbm,
    up_hbm,
    down_hbm,
    next_rows_ref,
    next_queue_ref,
    gain_ref,
    skip_ref,
    up_ref,
    down_ref,
    rows_in,
    queue_in,
    outputs,
    total,
    normed,
    hidden,
    load_sem,
    queue_send,
    queue_recv,
    rows_send,
    rows_recv,
    hold_sem,
    relay,
    relay_send,
    relay_recv,
    early_in,
    early_send,
    early_recv,
):
    me = lax.axis_index("section")
    half = sections // 2
    right = lax.rem(me + 1, sections)
    left = lax.rem(me + sections - 1, sections)
    mirror = sections - 1 - me
    encoder = me < half
    decoder = me >= half
    far = jnp.logical_and(me < half // 2, lax.rem(me, 2) == 1)
    near = jnp.logical_and(encoder, jnp.logical_not(far))
    row_count, width = rows_hbm.shape[1:]
    hidden_width = up_ref.shape[1]

    load_up = pltpu.make_async_copy(up_hbm.at[0], up_ref, load_sem.at[0])
    load_down = pltpu.make_async_copy(down_hbm.at[0], down_ref, load_sem.at[1])
    load_rows = pltpu.make_async_copy(rows_hbm.at[0], rows_in.at[0], load_sem.at[2])
    load_skip = pltpu.make_async_copy(skip_hbm.at[0], skip_ref, load_sem.at[3])
    load_queue = pltpu.make_async_copy(queue_hbm.at[0], queue_in.at[0], load_sem.at[4])
    load_gain = pltpu.make_async_copy(gain_hbm, gain_ref, load_sem.at[5])

    leader = half - 1
    holders = range(half // 2)
    holds = me < half // 2

    helper = leader - 2
    relayed = relay.shape[0]
    first, rest = pl.ds(0, relayed), pl.ds(relayed, row_count - relayed)

    def relay_copy(hop):
        return pltpu.make_async_remote_copy(
            src_ref=relay if hop else outputs.at[TICKS - 1, first],
            dst_ref=next_rows_ref.at[0, first] if hop else relay,
            send_sem=relay_send,
            recv_sem=relay_recv,
            device_id={"section": half if hop else helper},
            device_id_type=MESH,
        )

    direct_copy = pltpu.make_async_remote_copy(
        src_ref=outputs.at[TICKS - 1, rest],
        dst_ref=next_rows_ref.at[0, rest],
        send_sem=rows_send.at[TICKS - 1],
        recv_sem=rows_recv.at[TICKS - 1],
        device_id={"section": half},
        device_id_type=MESH,
    )

    ahead = jnp.logical_or(me == half - 4, me == half - 2)
    target = jnp.logical_or(me == half + 1, me == half + 3)
    after = jnp.logical_or(me == half - 3, me == half - 1)
    across = jnp.where(me == half + 1, half + 3, half + 1)
    via = jnp.where(me == half - 4, half + 1, half + 3)
    served = jnp.where(me == half + 1, half - 4, half - 2)
    early = early_in.shape[0]
    soon, later = pl.ds(0, early), pl.ds(early, row_count - early)

    def early_copy(hop):
        return pltpu.make_async_remote_copy(
            src_ref=early_in if hop else queue_hbm.at[0, soon],
            dst_ref=queue_in.at[1, soon] if hop else early_in,
            send_sem=early_send.at[hop],
            recv_sem=early_recv.at[hop],
            device_id={"section": across if hop else via},
            device_id_type=MESH,
        )

    late_copy = pltpu.make_async_remote_copy(
        src_ref=queue_hbm.at[0, later],
        dst_ref=queue_in.at[1, later],
        send_sem=queue_send.at[0],
        recv_sem=queue_recv.at[0],
        device_id={"section": mirror},
        device_id_type=MESH,
    )

    def queue_copy(tick):
        source = queue_hbm.at[0] if tick == 0 else outputs.at[tick - 1]
        return pltpu.make_async_remote_copy(
            src_ref=source,
            dst_ref=next_queue_ref.at[0] if tick == TICKS - 1 else queue_in.at[tick + 1],
            send_sem=queue_send.at[tick],
            recv_sem=queue_recv.at[tick],
            device_id={"section": mirror},
            device_id_type=MESH,
        )

    def rows_copy(tick):
        return pltpu.make_async_remote_copy(
            src_ref=outputs.at[tick],
            dst_ref=next_rows_ref.at[0] if tick == TICKS - 1 else rows_in.at[tick + 1],
            send_sem=rows_send.at[tick],
            recv_sem=rows_recv.at[tick],
            device_id={"section": right},
            device_id_type=MESH,
        )

    barrier = pltpu.get_barrier_semaphore()

    def greet(sem, peer):
        pl.semaphore_signal(sem, inc=1, device_id={"section": peer}, device_id_type=MESH)

    @pl.when(target)
    def _():
        greet(barrier, served)
        greet(barrier, across)

    @pl.when(jnp.logical_and(decoder, jnp.logical_not(target)))
    def _():
        greet(barrier, mirror)

    @pl.when(jnp.logical_not(after))
    def _():
        greet(barrier, left)

    @pl.when(ahead)
    def _():
        greet(barrier, mirror)
        greet(barrier, right)

    @pl.when(jnp.logical_or(holds, me == helper))
    def _():
        greet(barrier, leader)

    @pl.when(me == half)
    def _():
        greet(barrier, helper)

    @pl.when(ahead)
    def _():
        pl.semaphore_wait(barrier, 1)
        early_copy(0).start()

    @pl.when(me == helper)
    def _():
        pl.semaphore_wait(barrier, 4)
        greet(hold_sem, left)

    @pl.when(me == leader)
    def _():
        pl.semaphore_wait(barrier, 4 + len(holders))
        greet(hold_sem, left)

    @pl.when(jnp.logical_and(me < half, jnp.logical_not(jnp.logical_or(ahead, after))))
    def _():
        pl.semaphore_wait(barrier, 2)

    @pl.when(target)
    def _():
        pl.semaphore_wait(barrier, 3)
        greet(hold_sem, mirror)

    @pl.when(jnp.logical_and(decoder, jnp.logical_not(target)))
    def _():
        pl.semaphore_wait(barrier, 1)

    @pl.when(jnp.logical_and(near, jnp.logical_not(ahead)))
    def _():
        queue_copy(0).start()

    load_rows.start()
    load_gain.start()
    load_up.start()
    load_down.start()

    @pl.when(decoder)
    def _():
        load_queue.start()
        load_skip.start()

    @pl.when(ahead)
    def _():
        pl.semaphore_wait(hold_sem, 2)
        late_copy.start()

    @pl.when(target)
    def _():
        early_copy(0).wait_recv()
        early_copy(1).start()

    for tick in range(TICKS):
        if tick == 0:
            load_rows.wait()
            load_gain.wait()

            @pl.when(decoder)
            def _():
                load_queue.wait()
                load_skip.wait()
        else:
            @pl.when(me != half)
            def _():
                rows_copy(tick - 1).wait_recv()

            if tick == 1:

                @pl.when(jnp.logical_and(decoder, jnp.logical_not(target)))
                def _():
                    queue_copy(0).wait_recv()

                @pl.when(target)
                def _():
                    early_copy(1).wait_recv()
                    late_copy.wait_recv()
            else:

                @pl.when(me > half)
                def _():
                    queue_copy(tick - 1).wait_recv()

            @pl.when(me == half)
            def _():
                queue_copy(tick).wait_recv()
                rows_in[tick] = next_queue_ref[0] if tick == TICKS - 1 else queue_in[tick + 1]

        @pl.when(encoder)
        def _():
            total[...] = rows_in[tick].astype(jnp.float32)

        @pl.when(decoder)
        def _():
            for start, size in spans(width, 256):
                columns = pl.ds(start, size)
                total[:, columns] = jnp.dot(
                    rows_in[tick], skip_ref[:width, columns], preferred_element_type=jnp.float32
                ) + jnp.dot(
                    queue_in[tick], skip_ref[width:, columns], preferred_element_type=jnp.float32
                )

        merged = total[...]
        center = jnp.mean(merged, axis=1, keepdims=True)
        spread = jnp.mean(jnp.square(merged - center), axis=1, keepdims=True)
        normed[...] = ((merged - center) * lax.rsqrt(spread + epsilon) * gain_ref[...]).astype(
            jnp.bfloat16
        )

        if tick == 0:
            load_up.wait()

        for start, size in spans(hidden_width, 512):
            columns = pl.ds(start, size)
            hidden[:, columns] = jax.nn.gelu(
                jnp.dot(normed[...], up_ref[:, columns], preferred_element_type=jnp.float32),
                approximate=True,
            ).astype(jnp.bfloat16)

        if tick == 0:
            load_down.wait()

        for start, size in spans(width, 256):
            columns = pl.ds(start, size)
            outputs[tick, :, columns] = (
                total[:, columns]
                + jnp.dot(hidden[...], down_ref[:, columns], preferred_element_type=jnp.float32)
            ).astype(jnp.bfloat16)

        if tick < TICKS - 1:

            @pl.when(me != half - 1)
            def _():
                rows_copy(tick).start()

            if tick == 0:

                @pl.when(far)
                def _():
                    queue_copy(0).start()

            now = encoder if tick < TICKS - 2 else jnp.logical_and(encoder, jnp.logical_not(holds))

            @pl.when(now)
            def _():
                queue_copy(tick + 1).start()
        else:

            @pl.when(me != leader)
            def _():
                rows_copy(tick).start()

            @pl.when(me == leader)
            def _():
                relay_copy(0).start()
                direct_copy.start()

    @pl.when(encoder)
    def _():
        next_queue_ref[0] = outputs[TICKS - 1]

    @pl.when(me == leader)
    def _():
        queue_copy(TICKS - 1).wait_send()
        for peer in holders:
            pl.semaphore_signal(hold_sem, inc=1, device_id={"section": peer}, device_id_type=MESH)

    @pl.when(holds)
    def _():
        pl.semaphore_wait(hold_sem, 1)
        queue_copy(TICKS - 1).start()

    @pl.when(me == helper)
    def _():
        relay_copy(0).wait_recv()
        relay_copy(1).start()

    @pl.when(me != half)
    def _():
        rows_copy(TICKS - 1).wait_recv()

    @pl.when(me == half)
    def _():
        direct_copy.wait_recv()
        relay_copy(1).wait_recv()

    @pl.when(me > half)
    def _():
        queue_copy(TICKS - 1).wait_recv()

    for tick in range(TICKS):
        unsent = encoder
        if tick == 0:
            unsent = jnp.logical_and(encoder, jnp.logical_not(ahead))
        elif tick == TICKS - 1:
            unsent = jnp.logical_and(encoder, me != leader)

        @pl.when(unsent)
        def _():
            queue_copy(tick).wait_send()

        if tick < TICKS - 1:

            @pl.when(me != half - 1)
            def _():
                rows_copy(tick).wait_send()
        else:

            @pl.when(me != leader)
            def _():
                rows_copy(tick).wait_send()

            @pl.when(me == leader)
            def _():
                relay_copy(0).wait_send()
                direct_copy.wait_send()

    @pl.when(me == helper)
    def _():
        relay_copy(1).wait_send()

    @pl.when(ahead)
    def _():
        early_copy(0).wait_send()
        late_copy.wait_send()

    @pl.when(target)
    def _():
        early_copy(1).wait_send()


def store(rows_ref, queue_ref, rows_hbm, queue_hbm, sem):
    copies = [
        pltpu.make_async_copy(rows_ref, rows_hbm, sem.at[0]),
        pltpu.make_async_copy(queue_ref, queue_hbm, sem.at[1]),
    ]
    for copy in copies:
        copy.start()
    for copy in copies:
        copy.wait()


def local(latent_rows, skip_queue, norm_gain, skip_weight, up_weight, down_weight):
    sections = lax.axis_size("section")
    _, row_count, width = latent_rows.shape
    hidden_width = up_weight.shape[2]
    shape = jax.ShapeDtypeStruct(latent_rows.shape, jnp.bfloat16)
    relayed = row_count // 32 * 16
    early = row_count // 64 * 16
    in_hbm = pl.BlockSpec(memory_space=pltpu.HBM)
    in_vmem = pl.BlockSpec(memory_space=pltpu.VMEM)
    results = pl.pallas_call(
        functools.partial(kernel, sections),
        out_shape=(shape, shape),
        in_specs=[in_hbm] * 6,
        out_specs=(in_vmem, in_vmem),
        scratch_shapes=[
            pltpu.VMEM((1, width), jnp.float32),
            pltpu.VMEM((2 * width, width), jnp.bfloat16),
            pltpu.VMEM((width, hidden_width), jnp.bfloat16),
            pltpu.VMEM((hidden_width, width), jnp.bfloat16),
            pltpu.VMEM((TICKS, row_count, width), jnp.bfloat16),
            pltpu.VMEM((TICKS, row_count, width), jnp.bfloat16),
            pltpu.VMEM((TICKS, row_count, width), jnp.bfloat16),
            pltpu.VMEM((row_count, width), jnp.float32),
            pltpu.VMEM((row_count, width), jnp.bfloat16),
            pltpu.VMEM((row_count, hidden_width), jnp.bfloat16),
            pltpu.SemaphoreType.DMA((6,)),
            pltpu.SemaphoreType.DMA((TICKS,)),
            pltpu.SemaphoreType.DMA((TICKS,)),
            pltpu.SemaphoreType.DMA((TICKS,)),
            pltpu.SemaphoreType.DMA((TICKS,)),
            pltpu.SemaphoreType.REGULAR,
            pltpu.VMEM((relayed, width), jnp.bfloat16),
            pltpu.SemaphoreType.DMA,
            pltpu.SemaphoreType.DMA,
            pltpu.VMEM((early, width), jnp.bfloat16),
            pltpu.SemaphoreType.DMA((2,)),
            pltpu.SemaphoreType.DMA((2,)),
        ],
        compiler_params=pltpu.CompilerParams(
            collective_id=0, has_side_effects=True, vmem_limit_bytes=52 << 20
        ),
    )(latent_rows, skip_queue, pltpu.with_memory_space_constraint(norm_gain, pltpu.HBM), skip_weight, up_weight, down_weight)
    return pl.pallas_call(
        store,
        out_shape=(shape, shape),
        in_specs=[pl.BlockSpec(memory_space=pl.ANY)] * 2,
        out_specs=(in_hbm, in_hbm),
        scratch_shapes=[pltpu.SemaphoreType.DMA((2,))],
        compiler_params=pltpu.CompilerParams(vmem_limit_bytes=1 << 20),
    )(*results)


def solution(mesh):
    return jax.shard_map(
        local,
        mesh=mesh,
        in_specs=(
            P(("groups", "section"), None, None),
            P(("groups", "section"), None, None),
            P("section", None),
            P("section", None, None),
            P("section", None, None),
            P("section", None, None),
        ),
        out_specs=(P(("groups", "section"), None, None), P(("groups", "section"), None, None)),
        check_vma=False,
    )
```

```python
import functools

import jax
import jax.numpy as jnp
from jax import lax
from jax.experimental import pallas as pl
from jax.experimental.pallas import tpu as pltpu
from jax.sharding import PartitionSpec as P

TICKS = 3


epsilon = 1e-06

MESH = pl.DeviceIdType.MESH


def spans(extent, step):
    return [(start, min(step, extent - start)) for start in range(0, extent, step)]


def kernel(
    sections,
    rows_hbm,
    queue_hbm,
    gain_hbm,
    skip_hbm,
    up_hbm,
    down_hbm,
    next_rows_ref,
    next_queue_ref,
    gain_ref,
    skip_ref,
    up_ref,
    down_ref,
    rows_in,
    queue_in,
    outputs,
    total,
    normed,
    hidden,
    load_sem,
    queue_send,
    queue_recv,
    rows_send,
    rows_recv,
    hold_sem,
    relay,
    relay_send,
    relay_recv,
):
    me = lax.axis_index("section")
    half = sections // 2
    right = lax.rem(me + 1, sections)
    left = lax.rem(me + sections - 1, sections)
    mirror = sections - 1 - me
    encoder = me < half
    decoder = me >= half
    far = jnp.logical_and(me < half // 2, lax.rem(me, 2) == 1)
    near = jnp.logical_and(encoder, jnp.logical_not(far))
    row_count, width = rows_hbm.shape[1:]
    hidden_width = up_ref.shape[1]

    load_up = pltpu.make_async_copy(up_hbm.at[0], up_ref, load_sem.at[0])
    load_down = pltpu.make_async_copy(down_hbm.at[0], down_ref, load_sem.at[1])
    load_rows = pltpu.make_async_copy(rows_hbm.at[0], rows_in.at[0], load_sem.at[2])
    load_skip = pltpu.make_async_copy(skip_hbm.at[0], skip_ref, load_sem.at[3])
    load_queue = pltpu.make_async_copy(queue_hbm.at[0], queue_in.at[0], load_sem.at[4])
    load_gain = pltpu.make_async_copy(gain_hbm, gain_ref, load_sem.at[5])

    leader = half - 1
    holders = range(half // 2)
    holds = me < half // 2

    helper = leader - 2
    relayed = relay.shape[0]
    first, rest = pl.ds(0, relayed), pl.ds(relayed, row_count - relayed)

    def relay_copy(hop):
        return pltpu.make_async_remote_copy(
            src_ref=relay if hop else outputs.at[TICKS - 1, first],
            dst_ref=next_rows_ref.at[0, first] if hop else relay,
            send_sem=relay_send,
            recv_sem=relay_recv,
            device_id={"section": half if hop else helper},
            device_id_type=MESH,
        )

    direct_copy = pltpu.make_async_remote_copy(
        src_ref=outputs.at[TICKS - 1, rest],
        dst_ref=next_rows_ref.at[0, rest],
        send_sem=rows_send.at[TICKS - 1],
        recv_sem=rows_recv.at[TICKS - 1],
        device_id={"section": half},
        device_id_type=MESH,
    )

    ahead, via = half - 4, half + 1
    target = sections - 1 - ahead
    early = row_count // 64 * 16
    soon, later = pl.ds(0, early), pl.ds(early, row_count - early)

    def early_copy(hop):
        return pltpu.make_async_remote_copy(
            src_ref=relay.at[soon] if hop else queue_hbm.at[0, soon],
            dst_ref=queue_in.at[1, soon] if hop else relay.at[soon],
            send_sem=relay_send,
            recv_sem=relay_recv,
            device_id={"section": target if hop else via},
            device_id_type=MESH,
        )

    late_copy = pltpu.make_async_remote_copy(
        src_ref=queue_hbm.at[0, later],
        dst_ref=queue_in.at[1, later],
        send_sem=queue_send.at[0],
        recv_sem=queue_recv.at[0],
        device_id={"section": target},
        device_id_type=MESH,
    )

    def queue_copy(tick):
        source = queue_hbm.at[0] if tick == 0 else outputs.at[tick - 1]
        return pltpu.make_async_remote_copy(
            src_ref=source,
            dst_ref=next_queue_ref.at[0] if tick == TICKS - 1 else queue_in.at[tick + 1],
            send_sem=queue_send.at[tick],
            recv_sem=queue_recv.at[tick],
            device_id={"section": mirror},
            device_id_type=MESH,
        )

    def rows_copy(tick):
        return pltpu.make_async_remote_copy(
            src_ref=outputs.at[tick],
            dst_ref=next_rows_ref.at[0] if tick == TICKS - 1 else rows_in.at[tick + 1],
            send_sem=rows_send.at[tick],
            recv_sem=rows_recv.at[tick],
            device_id={"section": right},
            device_id_type=MESH,
        )

    barrier = pltpu.get_barrier_semaphore()

    def greet(sem, peer):
        pl.semaphore_signal(sem, inc=1, device_id={"section": peer}, device_id_type=MESH)

    @pl.when(me == via)
    def _():
        greet(barrier, ahead)

    @pl.when(jnp.logical_and(decoder, me != target))
    def _():
        greet(barrier, mirror)

    @pl.when(me == target)
    def _():
        greet(barrier, via)

    @pl.when(me != helper)
    def _():
        greet(barrier, left)

    @pl.when(me == ahead)
    def _():
        greet(barrier, target)
        greet(barrier, helper)

    @pl.when(jnp.logical_or(holds, me == helper))
    def _():
        greet(barrier, leader)

    @pl.when(me == half)
    def _():
        greet(barrier, helper)

    @pl.when(me == ahead)
    def _():
        pl.semaphore_wait(barrier, 1)
        early_copy(0).start()

    @pl.when(me == helper)
    def _():
        pl.semaphore_wait(barrier, 4)
        greet(hold_sem, ahead)

    @pl.when(me == leader)
    def _():
        pl.semaphore_wait(barrier, 3 + len(holders))

    @pl.when(
        jnp.logical_and(
            jnp.logical_and(encoder, me != ahead), jnp.logical_and(me != helper, me != leader)
        )
    )
    def _():
        pl.semaphore_wait(barrier, 2)

    @pl.when(me == target)
    def _():
        pl.semaphore_wait(barrier, 2)
        greet(hold_sem, ahead)

    @pl.when(me == via)
    def _():
        pl.semaphore_wait(barrier, 2)

    @pl.when(jnp.logical_and(decoder, jnp.logical_and(me != target, me != via)))
    def _():
        pl.semaphore_wait(barrier, 1)

    @pl.when(jnp.logical_and(near, me != ahead))
    def _():
        queue_copy(0).start()

    load_rows.start()
    load_gain.start()
    load_up.start()
    load_down.start()

    @pl.when(decoder)
    def _():
        load_queue.start()
        load_skip.start()

    @pl.when(me == ahead)
    def _():
        pl.semaphore_wait(hold_sem, 2)
        late_copy.start()

    @pl.when(me == via)
    def _():
        early_copy(0).wait_recv()
        early_copy(1).start()

    for tick in range(TICKS):
        if tick == 0:
            load_rows.wait()
            load_gain.wait()

            @pl.when(decoder)
            def _():
                load_queue.wait()
                load_skip.wait()
        else:
            @pl.when(me != half)
            def _():
                rows_copy(tick - 1).wait_recv()

            if tick == 1:

                @pl.when(jnp.logical_and(decoder, me != target))
                def _():
                    queue_copy(0).wait_recv()

                @pl.when(me == target)
                def _():
                    early_copy(1).wait_recv()
                    late_copy.wait_recv()
            else:

                @pl.when(me > half)
                def _():
                    queue_copy(tick - 1).wait_recv()

            @pl.when(me == half)
            def _():
                queue_copy(tick).wait_recv()
                rows_in[tick] = next_queue_ref[0] if tick == TICKS - 1 else queue_in[tick + 1]

        @pl.when(encoder)
        def _():
            total[...] = rows_in[tick].astype(jnp.float32)

        @pl.when(decoder)
        def _():
            for start, size in spans(width, 256):
                columns = pl.ds(start, size)
                total[:, columns] = jnp.dot(
                    rows_in[tick], skip_ref[:width, columns], preferred_element_type=jnp.float32
                ) + jnp.dot(
                    queue_in[tick], skip_ref[width:, columns], preferred_element_type=jnp.float32
                )

        merged = total[...]
        center = jnp.mean(merged, axis=1, keepdims=True)
        spread = jnp.mean(jnp.square(merged - center), axis=1, keepdims=True)
        normed[...] = ((merged - center) * lax.rsqrt(spread + epsilon) * gain_ref[...]).astype(
            jnp.bfloat16
        )

        if tick == 0:
            load_up.wait()

        for start, size in spans(hidden_width, 512):
            columns = pl.ds(start, size)
            hidden[:, columns] = jax.nn.gelu(
                jnp.dot(normed[...], up_ref[:, columns], preferred_element_type=jnp.float32),
                approximate=True,
            ).astype(jnp.bfloat16)

        if tick == 0:
            load_down.wait()

        for start, size in spans(width, 256):
            columns = pl.ds(start, size)
            outputs[tick, :, columns] = (
                total[:, columns]
                + jnp.dot(hidden[...], down_ref[:, columns], preferred_element_type=jnp.float32)
            ).astype(jnp.bfloat16)

        if tick < TICKS - 1:

            @pl.when(me != half - 1)
            def _():
                rows_copy(tick).start()

            if tick == 0:

                @pl.when(far)
                def _():
                    queue_copy(0).start()

            now = encoder if tick < TICKS - 2 else jnp.logical_and(encoder, jnp.logical_not(holds))

            @pl.when(now)
            def _():
                queue_copy(tick + 1).start()
        else:

            @pl.when(me != leader)
            def _():
                rows_copy(tick).start()

            @pl.when(me == leader)
            def _():
                relay_copy(0).start()
                direct_copy.start()

    @pl.when(encoder)
    def _():
        next_queue_ref[0] = outputs[TICKS - 1]

    @pl.when(me == leader)
    def _():
        queue_copy(TICKS - 1).wait_send()
        for peer in holders:
            pl.semaphore_signal(hold_sem, inc=1, device_id={"section": peer}, device_id_type=MESH)

    @pl.when(holds)
    def _():
        pl.semaphore_wait(hold_sem, 1)
        queue_copy(TICKS - 1).start()

    @pl.when(me == helper)
    def _():
        relay_copy(0).wait_recv()
        relay_copy(1).start()

    for tick in range(TICKS):
        unsent = encoder
        if tick == 0:
            unsent = jnp.logical_and(encoder, me != ahead)
        elif tick == TICKS - 1:
            unsent = jnp.logical_and(encoder, me != leader)

        @pl.when(unsent)
        def _():
            queue_copy(tick).wait_send()

        if tick < TICKS - 1:

            @pl.when(me != half - 1)
            def _():
                rows_copy(tick).wait_send()
        else:

            @pl.when(me != leader)
            def _():
                rows_copy(tick).wait_send()

            @pl.when(me == leader)
            def _():
                relay_copy(0).wait_send()
                direct_copy.wait_send()

    @pl.when(me == helper)
    def _():
        relay_copy(1).wait_send()

    @pl.when(me == ahead)
    def _():
        early_copy(0).wait_send()
        late_copy.wait_send()

    @pl.when(me == via)
    def _():
        early_copy(1).wait_send()

    @pl.when(me != half)
    def _():
        rows_copy(TICKS - 1).wait_recv()

    @pl.when(me == half)
    def _():
        direct_copy.wait_recv()
        relay_copy(1).wait_recv()

    @pl.when(me > half)
    def _():
        queue_copy(TICKS - 1).wait_recv()


def store(rows_ref, queue_ref, rows_hbm, queue_hbm, sem):
    copies = [
        pltpu.make_async_copy(rows_ref, rows_hbm, sem.at[0]),
        pltpu.make_async_copy(queue_ref, queue_hbm, sem.at[1]),
    ]
    for copy in copies:
        copy.start()
    for copy in copies:
        copy.wait()


def local(latent_rows, skip_queue, norm_gain, skip_weight, up_weight, down_weight):
    sections = lax.axis_size("section")
    _, row_count, width = latent_rows.shape
    hidden_width = up_weight.shape[2]
    shape = jax.ShapeDtypeStruct(latent_rows.shape, jnp.bfloat16)
    relayed = row_count * 9 // 256 * 16
    in_hbm = pl.BlockSpec(memory_space=pltpu.HBM)
    in_vmem = pl.BlockSpec(memory_space=pltpu.VMEM)
    results = pl.pallas_call(
        functools.partial(kernel, sections),
        out_shape=(shape, shape),
        in_specs=[in_hbm] * 6,
        out_specs=(in_vmem, in_vmem),
        scratch_shapes=[
            pltpu.VMEM((1, width), jnp.float32),
            pltpu.VMEM((2 * width, width), jnp.bfloat16),
            pltpu.VMEM((width, hidden_width), jnp.bfloat16),
            pltpu.VMEM((hidden_width, width), jnp.bfloat16),
            pltpu.VMEM((TICKS, row_count, width), jnp.bfloat16),
            pltpu.VMEM((TICKS, row_count, width), jnp.bfloat16),
            pltpu.VMEM((TICKS, row_count, width), jnp.bfloat16),
            pltpu.VMEM((row_count, width), jnp.float32),
            pltpu.VMEM((row_count, width), jnp.bfloat16),
            pltpu.VMEM((row_count, hidden_width), jnp.bfloat16),
            pltpu.SemaphoreType.DMA((6,)),
            pltpu.SemaphoreType.DMA((TICKS,)),
            pltpu.SemaphoreType.DMA((TICKS,)),
            pltpu.SemaphoreType.DMA((TICKS,)),
            pltpu.SemaphoreType.DMA((TICKS,)),
            pltpu.SemaphoreType.REGULAR,
            pltpu.VMEM((relayed, width), jnp.bfloat16),
            pltpu.SemaphoreType.DMA,
            pltpu.SemaphoreType.DMA,
        ],
        compiler_params=pltpu.CompilerParams(
            collective_id=0, has_side_effects=True, vmem_limit_bytes=52 << 20
        ),
    )(latent_rows, skip_queue, pltpu.with_memory_space_constraint(norm_gain, pltpu.HBM), skip_weight, up_weight, down_weight)
    return pl.pallas_call(
        store,
        out_shape=(shape, shape),
        in_specs=[pl.BlockSpec(memory_space=pl.ANY)] * 2,
        out_specs=(in_hbm, in_hbm),
        scratch_shapes=[pltpu.SemaphoreType.DMA((2,))],
        compiler_params=pltpu.CompilerParams(vmem_limit_bytes=1 << 20),
    )(*results)


def solution(mesh):
    return jax.shard_map(
        local,
        mesh=mesh,
        in_specs=(
            P(("groups", "section"), None, None),
            P(("groups", "section"), None, None),
            P("section", None),
            P("section", None, None),
            P("section", None, None),
            P("section", None, None),
        ),
        out_specs=(P(("groups", "section"), None, None), P(("groups", "section"), None, None)),
        check_vma=False,
    )
```

```python
import functools

import jax
import jax.numpy as jnp
from jax import lax
from jax.experimental import pallas as pl
from jax.experimental.pallas import tpu as pltpu
from jax.sharding import PartitionSpec as P

TICKS = 3


epsilon = 1e-06

MESH = pl.DeviceIdType.MESH


def spans(extent, step):
    return [(start, min(step, extent - start)) for start in range(0, extent, step)]


def kernel(
    sections,
    rows_hbm,
    queue_hbm,
    gain_hbm,
    skip_hbm,
    up_hbm,
    down_hbm,
    next_rows_ref,
    next_queue_ref,
    gain_ref,
    skip_ref,
    up_ref,
    down_ref,
    rows_in,
    queue_in,
    outputs,
    total,
    normed,
    hidden,
    load_sem,
    queue_send,
    queue_recv,
    rows_send,
    rows_recv,
    hold_sem,
    relay,
    relay_send,
    relay_recv,
):
    me = lax.axis_index("section")
    half = sections // 2
    right = lax.rem(me + 1, sections)
    left = lax.rem(me + sections - 1, sections)
    mirror = sections - 1 - me
    encoder = me < half
    decoder = me >= half
    far = jnp.logical_and(me < half // 2, lax.rem(me, 2) == 1)
    near = jnp.logical_and(encoder, jnp.logical_not(far))
    row_count, width = rows_hbm.shape[1:]
    hidden_width = up_ref.shape[1]

    load_up = pltpu.make_async_copy(up_hbm.at[0], up_ref, load_sem.at[0])
    load_down = pltpu.make_async_copy(down_hbm.at[0], down_ref, load_sem.at[1])
    load_rows = pltpu.make_async_copy(rows_hbm.at[0], rows_in.at[0], load_sem.at[2])
    load_skip = pltpu.make_async_copy(skip_hbm.at[0], skip_ref, load_sem.at[3])
    load_queue = pltpu.make_async_copy(queue_hbm.at[0], queue_in.at[0], load_sem.at[4])
    load_gain = pltpu.make_async_copy(gain_hbm, gain_ref, load_sem.at[5])

    leader = half - 1
    holders = range(half // 2)
    holds = me < half // 2

    helper = leader - 2
    relayed = relay.shape[0]
    first, rest = pl.ds(0, relayed), pl.ds(relayed, row_count - relayed)

    def relay_copy(hop):
        return pltpu.make_async_remote_copy(
            src_ref=relay if hop else outputs.at[TICKS - 1, first],
            dst_ref=next_rows_ref.at[0, first] if hop else relay,
            send_sem=relay_send,
            recv_sem=relay_recv,
            device_id={"section": half if hop else helper},
            device_id_type=MESH,
        )

    direct_copy = pltpu.make_async_remote_copy(
        src_ref=outputs.at[TICKS - 1, rest],
        dst_ref=next_rows_ref.at[0, rest],
        send_sem=rows_send.at[TICKS - 1],
        recv_sem=rows_recv.at[TICKS - 1],
        device_id={"section": half},
        device_id_type=MESH,
    )

    ahead, via = half - 4, half + 1
    target = sections - 1 - ahead
    early = row_count // 64 * 16
    soon, later = pl.ds(0, early), pl.ds(early, row_count - early)

    def early_copy(hop):
        return pltpu.make_async_remote_copy(
            src_ref=relay.at[soon] if hop else queue_hbm.at[0, soon],
            dst_ref=queue_in.at[1, soon] if hop else relay.at[soon],
            send_sem=relay_send,
            recv_sem=relay_recv,
            device_id={"section": target if hop else via},
            device_id_type=MESH,
        )

    late_copy = pltpu.make_async_remote_copy(
        src_ref=queue_hbm.at[0, later],
        dst_ref=queue_in.at[1, later],
        send_sem=queue_send.at[0],
        recv_sem=queue_recv.at[0],
        device_id={"section": target},
        device_id_type=MESH,
    )

    def queue_copy(tick):
        source = queue_hbm.at[0] if tick == 0 else outputs.at[tick - 1]
        return pltpu.make_async_remote_copy(
            src_ref=source,
            dst_ref=next_queue_ref.at[0] if tick == TICKS - 1 else queue_in.at[tick + 1],
            send_sem=queue_send.at[tick],
            recv_sem=queue_recv.at[tick],
            device_id={"section": mirror},
            device_id_type=MESH,
        )

    def rows_copy(tick):
        return pltpu.make_async_remote_copy(
            src_ref=outputs.at[tick],
            dst_ref=next_rows_ref.at[0] if tick == TICKS - 1 else rows_in.at[tick + 1],
            send_sem=rows_send.at[tick],
            recv_sem=rows_recv.at[tick],
            device_id={"section": right},
            device_id_type=MESH,
        )

    barrier = pltpu.get_barrier_semaphore()

    def greet(sem, peer):
        pl.semaphore_signal(sem, inc=1, device_id={"section": peer}, device_id_type=MESH)

    @pl.when(me == via)
    def _():
        greet(barrier, ahead)

    @pl.when(jnp.logical_and(decoder, me != target))
    def _():
        greet(barrier, mirror)

    @pl.when(me == target)
    def _():
        greet(barrier, via)

    @pl.when(me != helper)
    def _():
        greet(barrier, left)

    @pl.when(me == ahead)
    def _():
        greet(barrier, target)
        greet(barrier, helper)

    @pl.when(jnp.logical_or(holds, me == helper))
    def _():
        greet(barrier, leader)

    @pl.when(me == half)
    def _():
        greet(barrier, helper)

    @pl.when(me == ahead)
    def _():
        pl.semaphore_wait(barrier, 1)
        early_copy(0).start()

    @pl.when(me == helper)
    def _():
        pl.semaphore_wait(barrier, 4)
        greet(hold_sem, ahead)

    @pl.when(me == leader)
    def _():
        pl.semaphore_wait(barrier, 3 + len(holders))

    @pl.when(
        jnp.logical_and(
            jnp.logical_and(encoder, me != ahead), jnp.logical_and(me != helper, me != leader)
        )
    )
    def _():
        pl.semaphore_wait(barrier, 2)

    @pl.when(me == target)
    def _():
        pl.semaphore_wait(barrier, 2)
        greet(hold_sem, ahead)

    @pl.when(me == via)
    def _():
        pl.semaphore_wait(barrier, 2)

    @pl.when(jnp.logical_and(decoder, jnp.logical_and(me != target, me != via)))
    def _():
        pl.semaphore_wait(barrier, 1)

    @pl.when(jnp.logical_and(near, me != ahead))
    def _():
        queue_copy(0).start()

    load_rows.start()
    load_gain.start()
    load_up.start()
    load_down.start()

    @pl.when(decoder)
    def _():
        load_queue.start()
        load_skip.start()

    @pl.when(me == ahead)
    def _():
        pl.semaphore_wait(hold_sem, 2)
        late_copy.start()

    @pl.when(me == via)
    def _():
        early_copy(0).wait_recv()
        early_copy(1).start()

    for tick in range(TICKS):
        if tick == 0:
            load_rows.wait()
            load_gain.wait()

            @pl.when(decoder)
            def _():
                load_queue.wait()
                load_skip.wait()
        else:
            @pl.when(me != half)
            def _():
                rows_copy(tick - 1).wait_recv()

            if tick == 1:

                @pl.when(jnp.logical_and(decoder, me != target))
                def _():
                    queue_copy(0).wait_recv()

                @pl.when(me == target)
                def _():
                    early_copy(1).wait_recv()
                    late_copy.wait_recv()
            else:

                @pl.when(me > half)
                def _():
                    queue_copy(tick - 1).wait_recv()

            @pl.when(me == half)
            def _():
                queue_copy(tick).wait_recv()
                rows_in[tick] = next_queue_ref[0] if tick == TICKS - 1 else queue_in[tick + 1]

        @pl.when(encoder)
        def _():
            total[...] = rows_in[tick].astype(jnp.float32)

        @pl.when(decoder)
        def _():
            for start, size in spans(width, 256):
                columns = pl.ds(start, size)
                total[:, columns] = jnp.dot(
                    rows_in[tick], skip_ref[:width, columns], preferred_element_type=jnp.float32
                ) + jnp.dot(
                    queue_in[tick], skip_ref[width:, columns], preferred_element_type=jnp.float32
                )

        merged = total[...]
        center = jnp.mean(merged, axis=1, keepdims=True)
        spread = jnp.mean(jnp.square(merged - center), axis=1, keepdims=True)
        normed[...] = ((merged - center) * lax.rsqrt(spread + epsilon) * gain_ref[...]).astype(
            jnp.bfloat16
        )

        if tick == 0:
            load_up.wait()

        for start, size in spans(hidden_width, 512):
            columns = pl.ds(start, size)
            hidden[:, columns] = jax.nn.gelu(
                jnp.dot(normed[...], up_ref[:, columns], preferred_element_type=jnp.float32),
                approximate=True,
            ).astype(jnp.bfloat16)

        if tick == 0:
            load_down.wait()

        for start, size in spans(width, 256):
            columns = pl.ds(start, size)
            outputs[tick, :, columns] = (
                total[:, columns]
                + jnp.dot(hidden[...], down_ref[:, columns], preferred_element_type=jnp.float32)
            ).astype(jnp.bfloat16)

        if tick < TICKS - 1:

            @pl.when(me != half - 1)
            def _():
                rows_copy(tick).start()

            if tick == 0:

                @pl.when(far)
                def _():
                    queue_copy(0).start()

            now = encoder
            if tick == TICKS - 2:
                now = jnp.logical_and(encoder, jnp.logical_not(jnp.logical_or(holds, me == helper)))

            @pl.when(now)
            def _():
                queue_copy(tick + 1).start()
        else:

            @pl.when(me != leader)
            def _():
                rows_copy(tick).start()

            @pl.when(me == leader)
            def _():
                relay_copy(0).start()
                direct_copy.start()

    @pl.when(encoder)
    def _():
        next_queue_ref[0] = outputs[TICKS - 1]

    @pl.when(me == leader)
    def _():
        queue_copy(TICKS - 1).wait_send()
        for peer in holders:
            pl.semaphore_signal(hold_sem, inc=1, device_id={"section": peer}, device_id_type=MESH)

    @pl.when(holds)
    def _():
        pl.semaphore_wait(hold_sem, 1)
        queue_copy(TICKS - 1).start()

    @pl.when(me == helper)
    def _():
        relay_copy(0).wait_recv()
        relay_copy(1).start()
        queue_copy(TICKS - 1).start()

    @pl.when(me != half)
    def _():
        rows_copy(TICKS - 1).wait_recv()

    @pl.when(me == half)
    def _():
        direct_copy.wait_recv()
        relay_copy(1).wait_recv()

    @pl.when(me > half)
    def _():
        queue_copy(TICKS - 1).wait_recv()

    for tick in range(TICKS):
        unsent = encoder
        if tick == 0:
            unsent = jnp.logical_and(encoder, me != ahead)
        elif tick == TICKS - 1:
            unsent = jnp.logical_and(encoder, me != leader)

        @pl.when(unsent)
        def _():
            queue_copy(tick).wait_send()

        if tick < TICKS - 1:

            @pl.when(me != half - 1)
            def _():
                rows_copy(tick).wait_send()
        else:

            @pl.when(me != leader)
            def _():
                rows_copy(tick).wait_send()

            @pl.when(me == leader)
            def _():
                relay_copy(0).wait_send()
                direct_copy.wait_send()

    @pl.when(me == helper)
    def _():
        relay_copy(1).wait_send()

    @pl.when(me == ahead)
    def _():
        early_copy(0).wait_send()
        late_copy.wait_send()

    @pl.when(me == via)
    def _():
        early_copy(1).wait_send()


def store(rows_ref, queue_ref, rows_hbm, queue_hbm, sem):
    copies = [
        pltpu.make_async_copy(rows_ref, rows_hbm, sem.at[0]),
        pltpu.make_async_copy(queue_ref, queue_hbm, sem.at[1]),
    ]
    for copy in copies:
        copy.start()
    for copy in copies:
        copy.wait()


def local(latent_rows, skip_queue, norm_gain, skip_weight, up_weight, down_weight):
    sections = lax.axis_size("section")
    _, row_count, width = latent_rows.shape
    hidden_width = up_weight.shape[2]
    shape = jax.ShapeDtypeStruct(latent_rows.shape, jnp.bfloat16)
    relayed = row_count * 9 // 256 * 16
    in_hbm = pl.BlockSpec(memory_space=pltpu.HBM)
    in_vmem = pl.BlockSpec(memory_space=pltpu.VMEM)
    results = pl.pallas_call(
        functools.partial(kernel, sections),
        out_shape=(shape, shape),
        in_specs=[in_hbm] * 6,
        out_specs=(in_vmem, in_vmem),
        scratch_shapes=[
            pltpu.VMEM((1, width), jnp.float32),
            pltpu.VMEM((2 * width, width), jnp.bfloat16),
            pltpu.VMEM((width, hidden_width), jnp.bfloat16),
            pltpu.VMEM((hidden_width, width), jnp.bfloat16),
            pltpu.VMEM((TICKS, row_count, width), jnp.bfloat16),
            pltpu.VMEM((TICKS, row_count, width), jnp.bfloat16),
            pltpu.VMEM((TICKS, row_count, width), jnp.bfloat16),
            pltpu.VMEM((row_count, width), jnp.float32),
            pltpu.VMEM((row_count, width), jnp.bfloat16),
            pltpu.VMEM((row_count, hidden_width), jnp.bfloat16),
            pltpu.SemaphoreType.DMA((6,)),
            pltpu.SemaphoreType.DMA((TICKS,)),
            pltpu.SemaphoreType.DMA((TICKS,)),
            pltpu.SemaphoreType.DMA((TICKS,)),
            pltpu.SemaphoreType.DMA((TICKS,)),
            pltpu.SemaphoreType.REGULAR,
            pltpu.VMEM((relayed, width), jnp.bfloat16),
            pltpu.SemaphoreType.DMA,
            pltpu.SemaphoreType.DMA,
        ],
        compiler_params=pltpu.CompilerParams(
            collective_id=0, has_side_effects=True, vmem_limit_bytes=52 << 20
        ),
    )(latent_rows, skip_queue, pltpu.with_memory_space_constraint(norm_gain, pltpu.HBM), skip_weight, up_weight, down_weight)
    return pl.pallas_call(
        store,
        out_shape=(shape, shape),
        in_specs=[pl.BlockSpec(memory_space=pl.ANY)] * 2,
        out_specs=(in_hbm, in_hbm),
        scratch_shapes=[pltpu.SemaphoreType.DMA((2,))],
        compiler_params=pltpu.CompilerParams(vmem_limit_bytes=1 << 20),
    )(*results)


def solution(mesh):
    return jax.shard_map(
        local,
        mesh=mesh,
        in_specs=(
            P(("groups", "section"), None, None),
            P(("groups", "section"), None, None),
            P("section", None),
            P("section", None, None),
            P("section", None, None),
            P("section", None, None),
        ),
        out_specs=(P(("groups", "section"), None, None), P(("groups", "section"), None, None)),
        check_vma=False,
    )
```

```python
import functools

import jax
import jax.numpy as jnp
from jax import lax
from jax.experimental import pallas as pl
from jax.experimental.pallas import tpu as pltpu
from jax.sharding import PartitionSpec as P

TICKS = 3


epsilon = 1e-06

MESH = pl.DeviceIdType.MESH


def spans(extent, step):
    return [(start, min(step, extent - start)) for start in range(0, extent, step)]


def kernel(
    sections,
    rows_hbm,
    queue_hbm,
    gain_hbm,
    skip_hbm,
    up_hbm,
    down_hbm,
    next_rows_ref,
    next_queue_ref,
    gain_ref,
    skip_ref,
    up_ref,
    down_ref,
    rows_in,
    queue_in,
    outputs,
    total,
    normed,
    hidden,
    load_sem,
    queue_send,
    queue_recv,
    rows_send,
    rows_recv,
    hold_sem,
    relay,
    relay_send,
    relay_recv,
):
    me = lax.axis_index("section")
    half = sections // 2
    right = lax.rem(me + 1, sections)
    left = lax.rem(me + sections - 1, sections)
    mirror = sections - 1 - me
    encoder = me < half
    decoder = me >= half
    row_count, width = rows_hbm.shape[1:]
    hidden_width = up_ref.shape[1]

    load_up = pltpu.make_async_copy(up_hbm.at[0], up_ref, load_sem.at[0])
    load_down = pltpu.make_async_copy(down_hbm.at[0], down_ref, load_sem.at[1])
    load_rows = pltpu.make_async_copy(rows_hbm.at[0], rows_in.at[0], load_sem.at[2])
    load_skip = pltpu.make_async_copy(skip_hbm.at[0], skip_ref, load_sem.at[3])
    load_queue = pltpu.make_async_copy(queue_hbm.at[0], queue_in.at[0], load_sem.at[4])
    load_gain = pltpu.make_async_copy(gain_hbm, gain_ref, load_sem.at[5])

    leader = half - 1
    holders = range(half // 2)
    holds = me < half // 2

    helper = leader - 2
    relayed = relay.shape[0]
    first, rest = pl.ds(0, relayed), pl.ds(relayed, row_count - relayed)

    def relay_copy(hop):
        return pltpu.make_async_remote_copy(
            src_ref=relay if hop else outputs.at[TICKS - 1, first],
            dst_ref=next_rows_ref.at[0, first] if hop else relay,
            send_sem=relay_send,
            recv_sem=relay_recv,
            device_id={"section": half if hop else helper},
            device_id_type=MESH,
        )

    direct_copy = pltpu.make_async_remote_copy(
        src_ref=outputs.at[TICKS - 1, rest],
        dst_ref=next_rows_ref.at[0, rest],
        send_sem=rows_send.at[TICKS - 1],
        recv_sem=rows_recv.at[TICKS - 1],
        device_id={"section": half},
        device_id_type=MESH,
    )

    ahead, via = half - 4, half + 1
    target = sections - 1 - ahead
    early = row_count // 64 * 16
    soon, later = pl.ds(0, early), pl.ds(early, row_count - early)

    def early_copy(hop):
        return pltpu.make_async_remote_copy(
            src_ref=relay.at[soon] if hop else queue_hbm.at[0, soon],
            dst_ref=queue_in.at[1, soon] if hop else relay.at[soon],
            send_sem=relay_send,
            recv_sem=relay_recv,
            device_id={"section": target if hop else via},
            device_id_type=MESH,
        )

    late_copy = pltpu.make_async_remote_copy(
        src_ref=queue_hbm.at[0, later],
        dst_ref=queue_in.at[1, later],
        send_sem=queue_send.at[0],
        recv_sem=queue_recv.at[0],
        device_id={"section": target},
        device_id_type=MESH,
    )

    def queue_copy(tick):
        source = queue_hbm.at[0] if tick == 0 else outputs.at[tick - 1]
        return pltpu.make_async_remote_copy(
            src_ref=source,
            dst_ref=next_queue_ref.at[0] if tick == TICKS - 1 else queue_in.at[tick + 1],
            send_sem=queue_send.at[tick],
            recv_sem=queue_recv.at[tick],
            device_id={"section": mirror},
            device_id_type=MESH,
        )

    def rows_copy(tick):
        return pltpu.make_async_remote_copy(
            src_ref=outputs.at[tick],
            dst_ref=next_rows_ref.at[0] if tick == TICKS - 1 else rows_in.at[tick + 1],
            send_sem=rows_send.at[tick],
            recv_sem=rows_recv.at[tick],
            device_id={"section": right},
            device_id_type=MESH,
        )

    barrier = pltpu.get_barrier_semaphore()

    def greet(sem, peer):
        pl.semaphore_signal(sem, inc=1, device_id={"section": peer}, device_id_type=MESH)

    @pl.when(me == via)
    def _():
        greet(barrier, ahead)

    @pl.when(jnp.logical_and(decoder, me != target))
    def _():
        greet(barrier, mirror)

    @pl.when(me == target)
    def _():
        greet(barrier, via)

    @pl.when(me != helper)
    def _():
        greet(barrier, left)

    @pl.when(me == ahead)
    def _():
        greet(barrier, target)
        greet(barrier, helper)

    @pl.when(jnp.logical_or(holds, me == helper))
    def _():
        greet(barrier, leader)

    @pl.when(me == half)
    def _():
        greet(barrier, helper)

    @pl.when(me == ahead)
    def _():
        pl.semaphore_wait(barrier, 1)
        early_copy(0).start()

    @pl.when(me == helper)
    def _():
        pl.semaphore_wait(barrier, 4)
        greet(hold_sem, ahead)

    @pl.when(me == leader)
    def _():
        pl.semaphore_wait(barrier, 3 + len(holders))

    @pl.when(
        jnp.logical_and(
            jnp.logical_and(encoder, me != ahead), jnp.logical_and(me != helper, me != leader)
        )
    )
    def _():
        pl.semaphore_wait(barrier, 2)

    @pl.when(me == target)
    def _():
        pl.semaphore_wait(barrier, 2)
        greet(hold_sem, ahead)

    @pl.when(me == via)
    def _():
        pl.semaphore_wait(barrier, 2)

    @pl.when(jnp.logical_and(decoder, jnp.logical_and(me != target, me != via)))
    def _():
        pl.semaphore_wait(barrier, 1)

    @pl.when(jnp.logical_and(encoder, me != ahead))
    def _():
        queue_copy(0).start()

    load_rows.start()
    load_gain.start()
    load_up.start()
    load_down.start()

    @pl.when(decoder)
    def _():
        load_queue.start()
        load_skip.start()

    @pl.when(me == ahead)
    def _():
        pl.semaphore_wait(hold_sem, 2)
        late_copy.start()

    @pl.when(me == via)
    def _():
        early_copy(0).wait_recv()
        early_copy(1).start()

    for tick in range(TICKS):
        if tick == 0:
            load_rows.wait()
            load_gain.wait()

            @pl.when(decoder)
            def _():
                load_queue.wait()
                load_skip.wait()
        else:
            @pl.when(me != half)
            def _():
                rows_copy(tick - 1).wait_recv()

            if tick == 1:

                @pl.when(jnp.logical_and(decoder, me != target))
                def _():
                    queue_copy(0).wait_recv()

                @pl.when(me == target)
                def _():
                    early_copy(1).wait_recv()
                    late_copy.wait_recv()
            else:

                @pl.when(me > half)
                def _():
                    queue_copy(tick - 1).wait_recv()

            @pl.when(me == half)
            def _():
                queue_copy(tick).wait_recv()
                rows_in[tick] = next_queue_ref[0] if tick == TICKS - 1 else queue_in[tick + 1]

        @pl.when(encoder)
        def _():
            total[...] = rows_in[tick].astype(jnp.float32)

        @pl.when(decoder)
        def _():
            for start, size in spans(width, 256):
                columns = pl.ds(start, size)
                total[:, columns] = jnp.dot(
                    rows_in[tick], skip_ref[:width, columns], preferred_element_type=jnp.float32
                ) + jnp.dot(
                    queue_in[tick], skip_ref[width:, columns], preferred_element_type=jnp.float32
                )

        merged = total[...]
        center = jnp.mean(merged, axis=1, keepdims=True)
        spread = jnp.mean(jnp.square(merged - center), axis=1, keepdims=True)
        normed[...] = ((merged - center) * lax.rsqrt(spread + epsilon) * gain_ref[...]).astype(
            jnp.bfloat16
        )

        if tick == 0:
            load_up.wait()

        for start, size in spans(hidden_width, 512):
            columns = pl.ds(start, size)
            hidden[:, columns] = jax.nn.gelu(
                jnp.dot(normed[...], up_ref[:, columns], preferred_element_type=jnp.float32),
                approximate=True,
            ).astype(jnp.bfloat16)

        if tick == 0:
            load_down.wait()

        for start, size in spans(width, 256):
            columns = pl.ds(start, size)
            outputs[tick, :, columns] = (
                total[:, columns]
                + jnp.dot(hidden[...], down_ref[:, columns], preferred_element_type=jnp.float32)
            ).astype(jnp.bfloat16)

        if tick < TICKS - 1:

            @pl.when(me != half - 1)
            def _():
                rows_copy(tick).start()

            now = encoder if tick < TICKS - 2 else jnp.logical_and(encoder, jnp.logical_not(holds))

            @pl.when(now)
            def _():
                queue_copy(tick + 1).start()
        else:

            @pl.when(me != leader)
            def _():
                rows_copy(tick).start()

            @pl.when(me == leader)
            def _():
                relay_copy(0).start()
                direct_copy.start()

    @pl.when(encoder)
    def _():
        next_queue_ref[0] = outputs[TICKS - 1]

    @pl.when(me == leader)
    def _():
        queue_copy(TICKS - 1).wait_send()
        for peer in holders:
            pl.semaphore_signal(hold_sem, inc=1, device_id={"section": peer}, device_id_type=MESH)

    @pl.when(holds)
    def _():
        pl.semaphore_wait(hold_sem, 1)
        queue_copy(TICKS - 1).start()

    @pl.when(me == helper)
    def _():
        relay_copy(0).wait_recv()
        relay_copy(1).start()

    @pl.when(me != half)
    def _():
        rows_copy(TICKS - 1).wait_recv()

    @pl.when(me == half)
    def _():
        direct_copy.wait_recv()
        relay_copy(1).wait_recv()

    @pl.when(me > half)
    def _():
        queue_copy(TICKS - 1).wait_recv()

    for tick in range(TICKS):
        unsent = encoder
        if tick == 0:
            unsent = jnp.logical_and(encoder, me != ahead)
        elif tick == TICKS - 1:
            unsent = jnp.logical_and(encoder, me != leader)

        @pl.when(unsent)
        def _():
            queue_copy(tick).wait_send()

        if tick < TICKS - 1:

            @pl.when(me != half - 1)
            def _():
                rows_copy(tick).wait_send()
        else:

            @pl.when(me != leader)
            def _():
                rows_copy(tick).wait_send()

            @pl.when(me == leader)
            def _():
                relay_copy(0).wait_send()
                direct_copy.wait_send()

    @pl.when(me == helper)
    def _():
        relay_copy(1).wait_send()

    @pl.when(me == ahead)
    def _():
        early_copy(0).wait_send()
        late_copy.wait_send()

    @pl.when(me == via)
    def _():
        early_copy(1).wait_send()


def store(rows_ref, queue_ref, rows_hbm, queue_hbm, sem):
    copies = [
        pltpu.make_async_copy(rows_ref, rows_hbm, sem.at[0]),
        pltpu.make_async_copy(queue_ref, queue_hbm, sem.at[1]),
    ]
    for copy in copies:
        copy.start()
    for copy in copies:
        copy.wait()


def local(latent_rows, skip_queue, norm_gain, skip_weight, up_weight, down_weight):
    sections = lax.axis_size("section")
    _, row_count, width = latent_rows.shape
    hidden_width = up_weight.shape[2]
    shape = jax.ShapeDtypeStruct(latent_rows.shape, jnp.bfloat16)
    relayed = row_count * 9 // 256 * 16
    in_hbm = pl.BlockSpec(memory_space=pltpu.HBM)
    in_vmem = pl.BlockSpec(memory_space=pltpu.VMEM)
    results = pl.pallas_call(
        functools.partial(kernel, sections),
        out_shape=(shape, shape),
        in_specs=[in_hbm] * 6,
        out_specs=(in_vmem, in_vmem),
        scratch_shapes=[
            pltpu.VMEM((1, width), jnp.float32),
            pltpu.VMEM((2 * width, width), jnp.bfloat16),
            pltpu.VMEM((width, hidden_width), jnp.bfloat16),
            pltpu.VMEM((hidden_width, width), jnp.bfloat16),
            pltpu.VMEM((TICKS, row_count, width), jnp.bfloat16),
            pltpu.VMEM((TICKS, row_count, width), jnp.bfloat16),
            pltpu.VMEM((TICKS, row_count, width), jnp.bfloat16),
            pltpu.VMEM((row_count, width), jnp.float32),
            pltpu.VMEM((row_count, width), jnp.bfloat16),
            pltpu.VMEM((row_count, hidden_width), jnp.bfloat16),
            pltpu.SemaphoreType.DMA((6,)),
            pltpu.SemaphoreType.DMA((TICKS,)),
            pltpu.SemaphoreType.DMA((TICKS,)),
            pltpu.SemaphoreType.DMA((TICKS,)),
            pltpu.SemaphoreType.DMA((TICKS,)),
            pltpu.SemaphoreType.REGULAR,
            pltpu.VMEM((relayed, width), jnp.bfloat16),
            pltpu.SemaphoreType.DMA,
            pltpu.SemaphoreType.DMA,
        ],
        compiler_params=pltpu.CompilerParams(
            collective_id=0, has_side_effects=True, vmem_limit_bytes=52 << 20
        ),
    )(latent_rows, skip_queue, pltpu.with_memory_space_constraint(norm_gain, pltpu.HBM), skip_weight, up_weight, down_weight)
    return pl.pallas_call(
        store,
        out_shape=(shape, shape),
        in_specs=[pl.BlockSpec(memory_space=pl.ANY)] * 2,
        out_specs=(in_hbm, in_hbm),
        scratch_shapes=[pltpu.SemaphoreType.DMA((2,))],
        compiler_params=pltpu.CompilerParams(vmem_limit_bytes=1 << 20),
    )(*results)


def solution(mesh):
    return jax.shard_map(
        local,
        mesh=mesh,
        in_specs=(
            P(("groups", "section"), None, None),
            P(("groups", "section"), None, None),
            P("section", None),
            P("section", None, None),
            P("section", None, None),
            P("section", None, None),
        ),
        out_specs=(P(("groups", "section"), None, None), P(("groups", "section"), None, None)),
        check_vma=False,
    )
```
